256 devices in a mesh: ens: 4 (over x), gx: 8 (over z_lo, y), gy: 8 (over z_hi, core).
Axes of the slice: x: 4, y: 4, z: 8 (z_hi: 4, z_lo: 2; z = z_hi * 2 + z_lo), core: 2. Of those that a mesh axis runs over, the one named last changes fastest.
Arguments:
- forward_now: float32 [4, 3, 64, 256, 128], P('ens', None, 'gx', 'gy'), may hold values from -9 to 9
- forward_next: float32 [4, 3, 64, 256, 128], P('ens', None, 'gx', 'gy'), may hold values from -9 to 9
- adjoint_now: float32 [4, 3, 64, 256, 128], P('ens', None, 'gx', 'gy'), may hold values from -9 to 9
- adjoint_prev: float32 [4, 3, 64, 256, 128], P('ens', None, 'gx', 'gy'), may hold values from -9 to 9
- speed_p: float32 [64, 256, 128], P('gx', 'gy'), may hold values from 1.8 to 2.5
- speed_s: float32 [64, 256, 128], P('gx', 'gy'), may hold values from 0.6 to 1
- density: float32 [64, 256, 128], P('gx', 'gy'), may hold values from 1.5 to 3
- station_cells: int32 [4], P('ens'), may hold values from 0 to 2097151
- wavelets: float32 [4, 64], P('ens'), may hold values from -40 to 40
- receiver_cells: int32 [4, 48], P('ens'), may hold values from 0 to 2097151
- receiver_counts: int32 [4], P('ens'), may hold values from 1 to 48, 64 in all
- adjoint_traces: float32 [4, 48, 3, 64], P('ens'), may hold values from -6 to 6
- start_step: int32 [], replicated, may hold values from 0 to 62
Outputs:
- kernel_vp: float32 [64, 256, 128], P('gx', 'gy', 'ens')
- kernel_vs: float32 [64, 256, 128], P('gx', 'gy', 'ens')
- kernel_rho: float32 [64, 256, 128], P('gx', 'gy', 'ens')
The draws below stay inside these ranges and needn't reach their ends.
Inputs may be any that keep to these rules, and one draw needn't show every extreme that they name: `receiver_counts`: receiver counts sum to 64; the largest equals 48.
All inputs are finite; a program needn't handle non-finite values. No bound on the sum of `receiver_counts` on one device may be relied on, other than what follows from the above.
Results may differ from the reference program's by a relative error of at most 0.00012.
Values sent between devices are 32-bit elements; how exact they have to be, the bound alone decides.
No kernel may reach another device: no remote copies, remote signals or barrier semaphores. Data moves between devices by JAX's collectives and lax.ppermute only.
A program may use at most 64 MiB of HBM per device.

```python
import math
import jax
import jax.numpy as jnp
import numpy as np
from jax import lax

STEPS = 2
TIME = 64
R_MAX = 48
R_MEAN = 16
MEMBERS = 4
NX = 64
NY = 256
NZ = 128


def profile(count):
    places = jnp.arange(count, dtype=jnp.float32) + 0.5
    return jnp.clip(1.5 * jnp.sin(math.pi * places / count), 0.0, 1.0)


def static_part(key):
    keys = jax.random.split(key, 6)
    shape = (MEMBERS, 3, 1, 1, 1)
    level = 5.0
    swing = 0.15
    signs = (2 * jax.random.randint(keys[0], shape, 0, 2) - 1).astype(jnp.float32)
    amount = level * jax.random.uniform(keys[1], shape, jnp.float32, 0.8, 1.2)
    phase = jax.random.uniform(keys[2], shape, jnp.float32, 0.0, 2.0 * math.pi)
    wave_x = 2.0 * math.pi / jax.random.uniform(keys[3], shape, jnp.float32, 48.0, 96.0)
    wave_y = 2.0 * math.pi / jax.random.uniform(keys[4], shape, jnp.float32, 48.0, 96.0)
    wave_z = 2.0 * math.pi / jax.random.uniform(keys[5], shape, jnp.float32, 48.0, 96.0)
    coord_x = jnp.arange(NX, dtype=jnp.float32).reshape(1, 1, NX, 1, 1)
    coord_y = jnp.arange(NY, dtype=jnp.float32).reshape(1, 1, 1, NY, 1)
    coord_z = jnp.arange(NZ, dtype=jnp.float32).reshape(1, 1, 1, 1, NZ)
    envelope = profile(NX).reshape(1, 1, NX, 1, 1) * profile(NY).reshape(1, 1, 1, NY, 1) * profile(NZ).reshape(1, 1, 1, 1, NZ)
    angle_sum = wave_x * coord_x + wave_y * coord_y + wave_z * coord_z + phase
    return signs * amount * envelope * (1.0 + swing * jnp.cos(angle_sum))


def rough_part(key):
    shape = (MEMBERS, 3, NX, NY, NZ)
    return 0.25 * jax.random.truncated_normal(key, -4.0, 4.0, shape, jnp.float32)


def draw_forward_now(key, part):
    return static_part(jax.random.fold_in(key, 101)) + rough_part(jax.random.fold_in(key, 1))


def draw_forward_next(key, part):
    return static_part(jax.random.fold_in(key, 101)) + rough_part(jax.random.fold_in(key, 2))


def draw_adjoint_now(key, part):
    return static_part(jax.random.fold_in(key, 202)) + rough_part(jax.random.fold_in(key, 3))


def draw_adjoint_prev(key, part):
    return static_part(jax.random.fold_in(key, 202)) + rough_part(jax.random.fold_in(key, 4))


def place_ends(entries, stream_key, least, top_value):
    longest = entries.shape.index(max(entries.shape))
    spots = []
    for shift in (0, 1):
        where = [jax.random.randint(jax.random.fold_in(stream_key, axis), (), 0, length) for axis, length in enumerate(entries.shape)]
        where[longest] = (where[longest] + shift) % entries.shape[longest]
        spots.append(tuple(where))
    return entries.at[spots[0]].set(least).at[spots[1]].set(top_value)


def level_of(key, shape, pieces, low, top_value):
    factor_of = 1.0
    for position, blocks in pieces:
        steps = jax.random.uniform(jax.random.fold_in(jax.random.fold_in(key, 6), position), (blocks,), jnp.float32, low / len(pieces), top_value / len(pieces))
        factor_of = factor_of * jnp.repeat(jnp.exp(steps), shape[position] // blocks).reshape((-1,) + (1,) * (len(shape) - 1 - position))
    return factor_of


def length_profile(count, total, limit, skew):
    portions = [(1 << 20) // math.isqrt(rank ** skew) + 1 for rank in range(2, count + 1)]
    spare, given = total - limit - (count - 1), [1] * (count - 1)
    while spare > 0:
        movable = [i for i in range(count - 1) if given[i] < limit]
        pool, remaining = sum([portions[i] for i in movable]), spare
        for i in movable:
            more = min(limit - given[i], max(1, remaining * portions[i] // pool), spare)
            given[i] = given[i] + more
            spare = spare - more
    return np.array([limit] + given)


def ragged(stream_key, number_of, total, reach, skew):
    if number_of == 2:
        one = jax.random.randint(stream_key, (), max(1, total - reach), min(reach, total - 1) + 1)
        return jnp.stack([one, total - one])
    lengths = jnp.asarray(length_profile(number_of, total, reach, skew), jnp.int32)
    couples = (number_of - 1) // 2
    donor, sink = lengths[1:1 + 2 * couples:2], lengths[2:2 + 2 * couples:2]
    slack = jnp.minimum(donor - 1, reach - sink)
    shifted = jax.random.randint(jax.random.fold_in(stream_key, 1), (couples,), 0, 1 << 20) % (slack + 1)
    lengths = lengths.at[1:1 + 2 * couples:2].set(donor - shifted).at[2:2 + 2 * couples:2].set(sink + shifted)
    return lengths[jax.random.permutation(jax.random.fold_in(stream_key, 2), number_of)]


def noise(own_key, extent, deviation, most, cuts=(), kind=jnp.bfloat16):
    values = jax.random.normal(own_key, extent, jnp.float32) * deviation
    if len(cuts) > 0:
        values = level_of(own_key, extent, cuts, -0.22, 0.18) * values
    return jnp.clip(values, min=-most, max=most).astype(kind)


def setup_inputs(seed: int = 0) -> dict:
    seeds = jax.random.split(jax.random.key(seed), 14)
    forward_now = draw_forward_now(jax.random.fold_in(seeds[13], 71), 0)
    forward_next = draw_forward_next(jax.random.fold_in(seeds[13], 71), 0)
    adjoint_now = draw_adjoint_now(jax.random.fold_in(seeds[13], 71), 0)
    adjoint_prev = draw_adjoint_prev(jax.random.fold_in(seeds[13], 71), 0)
    speed_p = jnp.clip(1.8 + 0.70000005 * jax.random.uniform(seeds[4], (NX, NY, NZ), jnp.float32) ** level_of(seeds[4], (NX, NY, NZ), ((0, 8), (1, 8)), -0.2, 0.2), 1.8, 2.5)
    speed_s = jnp.clip(0.6 + 0.39999998 * jax.random.uniform(seeds[5], (NX, NY, NZ), jnp.float32) ** level_of(seeds[5], (NX, NY, NZ), ((0, 8), (1, 8)), -0.2, 0.2), 0.6, 1.0)
    density = jnp.clip(jnp.exp(math.log(3.0) - 0.6931472 * jax.random.uniform(seeds[6], (NX, NY, NZ), jnp.float32) ** level_of(seeds[6], (NX, NY, NZ), ((0, 8), (1, 8)), -0.2, 0.2)), 1.5, 3.0)
    station_cells = place_ends(jax.random.randint(seeds[7], (MEMBERS,), 0, NX * NY * NZ), jax.random.fold_in(seeds[7], 1), 0, (NX * NY * NZ) - 1).astype(jnp.int32)
    wavelets = noise(seeds[8], (MEMBERS, TIME), 10.0, 40.0, ((0, 4),), jnp.float32)
    receiver_cells = place_ends(jax.random.randint(seeds[9], (MEMBERS, R_MAX), 0, NX * NY * NZ), jax.random.fold_in(seeds[9], 1), 0, (NX * NY * NZ) - 1).astype(jnp.int32)
    receiver_counts = ragged(seeds[10], MEMBERS, R_MEAN * MEMBERS, R_MAX, 2).astype(jnp.int32)
    adjoint_traces = noise(seeds[11], (MEMBERS, R_MAX, 3, TIME), 1.0, 6.0, ((0, 4),), jnp.float32)
    start_step = jax.random.randint(seeds[12], (), 0, TIME - STEPS + 1).astype(jnp.int32)
    return {"forward_now": forward_now, "forward_next": forward_next, "adjoint_now": adjoint_now, "adjoint_prev": adjoint_prev, "speed_p": speed_p, "speed_s": speed_s, "density": density, "station_cells": station_cells, "wavelets": wavelets, "receiver_cells": receiver_cells, "receiver_counts": receiver_counts, "adjoint_traces": adjoint_traces, "start_step": start_step}


COEF = (0.8, -0.2, 4.0 / 105.0, -1.0 / 280.0)
STEP_DT = 0.25


def derive_valid(padded, axis, length_out):
    summed = None
    for offset in range(1, 5):
        upper = lax.slice_in_dim(padded, 4 + offset, 4 + offset + length_out, axis=axis)
        lower = lax.slice_in_dim(padded, 4 - offset, 4 - offset + length_out, axis=axis)
        term = COEF[offset - 1] * (upper - lower)
        summed = term if summed is None else summed + term
    return summed


def derive_padded(field, axis):
    widths = [(0, 0)] * field.ndim
    widths[axis] = (4, 4)
    return derive_valid(jnp.pad(field, widths), axis, field.shape[axis])


def stress_of(grads, lame_first, lame_second):
    trace = grads[0][0] + grads[1][1] + grads[2][2]
    stress = {}
    for i in range(3):
        for j in range(i, 3):
            value = lame_second * (grads[i][j] + grads[j][i])
            if i == j:
                value = lame_first * trace + value
            stress[(i, j)] = value
    return stress, trace


def pick(stress, i, j):
    return stress[(min(i, j), max(i, j))]


def mu_term(grads_a, grads_s):
    summed = None
    for i in range(3):
        for j in range(3):
            term = 0.5 * (grads_a[i][j] + grads_a[j][i]) * (grads_s[i][j] + grads_s[j][i])
            summed = term if summed is None else summed + term
    return summed


def place(cells, amounts, size_x, size_y, size_z, anchor_x, anchor_y, grid_y):
    plane = grid_y * size_z
    index_x = cells // plane - anchor_x
    index_y = (cells // size_z) % grid_y - anchor_y
    index_z = cells % size_z
    inside = (index_x >= 0) & (index_x < size_x) & (index_y >= 0) & (index_y < size_y)
    index_x = jnp.clip(index_x, 0, size_x - 1)
    index_y = jnp.clip(index_y, 0, size_y - 1)
    amounts = amounts * inside.astype(jnp.float32)[:, None]
    field = jnp.zeros((3, size_x, size_y, size_z), jnp.float32)
    for comp in range(3):
        field = field.at[comp, index_x, index_y, index_z].add(amounts[:, comp])
    return field


def forces(station_cell, wavelet, cells, counts, traces, moment, size_x, size_y, size_z, anchor_x, anchor_y, grid_y):
    amplitude = lax.dynamic_index_in_dim(wavelet, moment, 0, keepdims=False)
    zero = jnp.zeros((), jnp.float32)
    source_amounts = jnp.stack([zero, zero, amplitude])[None, :]
    source = place(station_cell[None], source_amounts, size_x, size_y, size_z, anchor_x, anchor_y, grid_y)
    live = (jnp.arange(cells.shape[0], dtype=jnp.int32) < counts).astype(jnp.float32)
    adjoint_amounts = lax.dynamic_index_in_dim(traces, moment, 2, keepdims=False) * live[:, None]
    adjoint = place(cells, adjoint_amounts, size_x, size_y, size_z, anchor_x, anchor_y, grid_y)
    return source, adjoint


def divergence_full(field, lame_first, lame_second):
    grads = [[derive_padded(field[j], i) for j in range(3)] for i in range(3)]
    stress, trace = stress_of(grads, lame_first, lame_second)
    result = []
    for i in range(3):
        value = derive_padded(pick(stress, i, 0), 0)
        value = value + derive_padded(pick(stress, i, 1), 1)
        value = value + derive_padded(pick(stress, i, 2), 2)
        result.append(value)
    return jnp.stack(result), grads, trace


def reference(forward_now, forward_next, adjoint_now, adjoint_prev, speed_p, speed_s, density, station_cells, wavelets, receiver_cells, receiver_counts, adjoint_traces, start_step):
    lame_first = density * (speed_p * speed_p - 2.0 * speed_s * speed_s)
    lame_second = density * speed_s * speed_s
    grid_x, grid_y, grid_z = speed_p.shape
    k_lam = jnp.zeros(speed_p.shape, jnp.float32)
    k_mu = jnp.zeros(speed_p.shape, jnp.float32)
    k_rho = jnp.zeros(speed_p.shape, jnp.float32)
    for member in range(forward_now.shape[0]):
        s_now, s_next = forward_now[member], forward_next[member]
        a_now, a_prev = adjoint_now[member], adjoint_prev[member]
        for step in range(STEPS):
            moment = start_step + (STEPS - 1 - step)
            source, adjoint = forces(station_cells[member], wavelets[member], receiver_cells[member], receiver_counts[member], adjoint_traces[member], moment, grid_x, grid_y, grid_z, 0, 0, grid_y)
            div_s, grads_s, trace_s = divergence_full(s_now, lame_first, lame_second)
            div_a, grads_a, trace_a = divergence_full(a_now, lame_first, lame_second)
            accel_s = (div_s + source) / density
            accel_a = (div_a + adjoint) / density
            k_lam = k_lam + trace_a * trace_s
            k_mu = k_mu + mu_term(grads_a, grads_s)
            k_rho = k_rho + (a_now[0] * accel_s[0] + a_now[1] * accel_s[1] + a_now[2] * accel_s[2])
            s_new = (2.0 * s_now - s_next) + (STEP_DT * STEP_DT) * accel_s
            a_new = (2.0 * a_now - a_prev) + (STEP_DT * STEP_DT) * accel_a
            s_next, s_now = s_now, s_new
            a_prev, a_now = a_now, a_new
    lam_scaled = STEP_DT * k_lam
    mu_scaled = STEP_DT * k_mu
    rho_scaled = STEP_DT * k_rho
    square_p = speed_p * speed_p
    square_s = speed_s * speed_s
    kernel_vp = 2.0 * density * square_p * lam_scaled
    kernel_vs = 2.0 * density * square_s * (mu_scaled - 2.0 * lam_scaled)
    kernel_rho = density * (rho_scaled + (square_p - 2.0 * square_s) * lam_scaled + square_s * mu_scaled)
    return kernel_vp, kernel_vs, kernel_rho
```

```python
import functools

import jax
import jax.numpy as jnp
from jax import lax
from jax.experimental import pallas as pl
from jax.experimental.pallas import tpu as pltpu
from jax.sharding import PartitionSpec as P

COEF = (0.8, -0.2, 4.0 / 105.0, -1.0 / 280.0)
STEP_DT = 0.25
F32 = jnp.float32
PAIRS = ((0, 0), (0, 1), (0, 2), (1, 1), (1, 2), (2, 2))
SLOT = {(0, 0): 0, (0, 1): 1, (0, 2): 2, (1, 0): 1, (1, 1): 3, (1, 2): 4, (2, 0): 2, (2, 1): 4, (2, 2): 5}
NX, NY, NZ = 8, 32, 128


def shapes(*dims):
    return jax.ShapeDtypeStruct(dims, F32)


def call(body, out_shape, scratch=(), smem=(), count=0, flops=0):
    specs = [
        pl.BlockSpec(memory_space=pltpu.SMEM if i in smem else pltpu.VMEM) for i in range(count)
    ]
    return pl.pallas_call(
        body,
        out_shape=out_shape,
        in_specs=specs,
        out_specs=jax.tree.map(lambda _: pl.BlockSpec(memory_space=pltpu.VMEM), out_shape),
        scratch_shapes=list(scratch),
        compiler_params=pltpu.CompilerParams(vmem_limit_bytes=40 << 20),
        cost_estimate=pl.CostEstimate(flops=flops, bytes_accessed=1 << 20, transcendentals=0),
    )


def even(axis):
    return lax.rem(lax.axis_index(axis), 2) == 0


def z_coefs():
    lane = lax.broadcasted_iota(jnp.int32, (8, NZ), 1)
    up = [jnp.where(lane < NZ - k, COEF[k - 1], 0.0).astype(F32) for k in range(1, 5)]
    down = [jnp.where(lane >= k, -COEF[k - 1], 0.0).astype(F32) for k in range(1, 5)]
    return up, down


def deriv_z(value, coefs):
    up, down = coefs
    rows = value.shape[0]
    full = value if rows % 8 == 0 else jnp.concatenate([value] * (8 // rows), axis=0)
    full = full.reshape(-1, 8, NZ)
    summed = None
    for k in range(1, 5):
        term = up[k - 1][None] * pltpu.roll(full, NZ - k, 2)
        term = term + down[k - 1][None] * pltpu.roll(full, k, 2)
        summed = term if summed is None else summed + term
    return summed.reshape(-1, NZ)[:rows]


def deriv_x(ref, c, x, y0, rows):
    summed = None
    for k in range(1, 5):
        term = COEF[k - 1] * (ref[c, x + k, pl.ds(y0, rows), :] - ref[c, x - k, pl.ds(y0, rows), :])
        summed = term if summed is None else summed + term
    return summed


def deriv_y(ref, c, x, y0, rows):
    summed = None
    for k in range(1, 5):
        term = COEF[k - 1] * (ref[c, x, pl.ds(y0 + k, rows), :] - ref[c, x, pl.ds(y0 - k, rows), :])
        summed = term if summed is None else summed + term
    return summed


def lame(vp, vs, rho):
    square_s = vs * vs
    return rho * (vp * vp - 2.0 * square_s), rho * square_s


def ordered(axis, got_even, got_odd, put):
    @pl.when(even(axis))
    def _():
        put(got_odd, got_even)

    @pl.when(jnp.logical_not(even(axis)))
    def _():
        put(got_even, got_odd)


def edge_rows(tile, out_e, out_o, base):
    upper = even("gy")
    for c in range(3):
        for x in range(NX):
            high, low = tile[c, x, NY - 8 :, :], tile[c, x, :8, :]
            out_e[base + c * NX + x] = jnp.where(upper, high, low)
            out_o[base + c * NX + x] = jnp.where(upper, low, high)


def pack_y(s, a, vp, vs, rho, out_e, out_o):
    edge_rows(s, out_e, out_o, 0)
    edge_rows(a, out_e, out_o, 3 * NX)
    upper = even("gy")
    for x in range(NX):
        lam, mu = lame(vp[x], vs[x], rho[x])
        high = jnp.concatenate([lam[NY - 4 :], mu[NY - 4 :]], axis=0)
        low = jnp.concatenate([lam[:4], mu[:4]], axis=0)
        out_e[6 * NX + x] = jnp.where(upper, high, low)
        out_o[6 * NX + x] = jnp.where(upper, low, high)


def pack_corner_rows(got_e, got_o, out_e, out_o, fields):
    def put(below, above):
        right = even("gx")
        for f in range(fields):
            for c in range(2):
                for i in range(4):
                    row = [None, None]
                    for side, x in ((0, i), (1, NX - 4 + i)):
                        at = (f * 3 + c) * NX + x
                        row[side] = jnp.concatenate([below[at][4:], above[at][:4]], axis=0)
                    slot = (f * 2 + c) * 4 + i
                    out_e[slot] = jnp.where(right, row[1], row[0])
                    out_o[slot] = jnp.where(right, row[0], row[1])

    ordered("gy", got_e, got_o, put)


def pack_x(got_e, got_o, vp, vs, rho, out_e, out_o):
    pack_corner_rows(got_e, got_o, out_e, out_o, 2)
    right = even("gx")
    for i in range(4):
        low = lame(vp[i], vs[i], rho[i])
        high = lame(vp[NX - 4 + i], vs[NX - 4 + i], rho[NX - 4 + i])
        for which in range(2):
            for part in range(4):
                rows = slice(8 * part, 8 * part + 8)
                slot = 16 + (which * 4 + i) * 4 + part
                out_e[slot] = jnp.where(right, high[which][rows], low[which][rows])
                out_o[slot] = jnp.where(right, low[which][rows], high[which][rows])


def pack_corner(got_e, got_o, out_e, out_o):
    pack_corner_rows(got_e, got_o, out_e, out_o, 1)


def fill_field(ext, tile, bulk, rows, base, corner, corner_base):
    ext[:, 8 : 8 + NX, 8 : 8 + NY, :] = tile[...]

    def put_x(left, right):
        ext[:, 0:8, 8 : 8 + NY, :] = left[...]
        ext[:, 8 + NX : 16 + NX, 8 : 8 + NY, :] = right[...]

    ordered("gx", bulk[0], bulk[1], put_x)

    def put_rows(below, above):
        for c in range(3):
            for x in range(NX):
                ext[c, 8 + x, 0:8, :] = below[base + c * NX + x]
                ext[c, 8 + x, 8 + NY : 16 + NY, :] = above[base + c * NX + x]

    ordered("gy", rows[0], rows[1], put_rows)

    def put_corner(left, right):
        for c in range(2):
            for i in range(4):
                at = corner_base + c * 4 + i
                ext[c, 4 + i, 4:8, :] = left[at][:4]
                ext[c, 4 + i, 8 + NY : 12 + NY, :] = left[at][4:]
                ext[c, 8 + NX + i, 4:8, :] = right[at][:4]
                ext[c, 8 + NX + i, 8 + NY : 12 + NY, :] = right[at][4:]

    ordered("gx", corner[0], corner[1], put_corner)


def fill_lame(lm, lmy, vp, vs, rho, rows, params):
    for x in range(NX):
        lam, mu = lame(vp[x], vs[x], rho[x])
        lm[0, 4 + x] = lam
        lm[1, 4 + x] = mu

    def put_x(left, right):
        for which in range(2):
            for i in range(4):
                for part in range(4):
                    at = 16 + (which * 4 + i) * 4 + part
                    lm[which, i, 8 * part : 8 * part + 8, :] = left[at]
                    lm[which, 4 + NX + i, 8 * part : 8 * part + 8, :] = right[at]

    ordered("gx", params[0], params[1], put_x)

    def put_rows(below, above):
        lmy[0] = below[6 * NX : 7 * NX]
        lmy[1] = above[6 * NX : 7 * NX]

    ordered("gy", rows[0], rows[1], put_rows)


def all_strain(ext, x, y0, rows, coefs):
    g = [[None] * 3 for _ in range(3)]
    for j in range(3):
        g[0][j] = deriv_x(ext, j, x, y0, rows)
        g[1][j] = deriv_y(ext, j, x, y0, rows)
        g[2][j] = deriv_z(ext[j, x, pl.ds(y0, rows), :], coefs)
    return [g[i][j] + g[j][i] for i, j in PAIRS]


def divergence(ext, lm, lmy, sx, sy, div, strain):
    coefs = z_coefs()

    def halo_plane(i, carry):
        x = jnp.where(i < 4, i, i + NX)
        xe = x + 4
        lam, mu = lm[0, x], lm[1, x]
        g00 = deriv_x(ext, 0, xe, 8, NY)
        g11 = deriv_y(ext, 1, xe, 8, NY)
        g22 = deriv_z(ext[2, xe, 8 : 8 + NY, :], coefs)
        sx[0, x] = lam * (g00 + g11 + g22) + mu * (g00 + g00)
        sx[1, x] = mu * (deriv_x(ext, 1, xe, 8, NY) + deriv_y(ext, 0, xe, 8, NY))
        sx[2, x] = mu * (
            deriv_x(ext, 2, xe, 8, NY) + deriv_z(ext[0, xe, 8 : 8 + NY, :], coefs)
        )
        return carry

    lax.fori_loop(0, 8, halo_plane, 0)

    def plane(x, carry):
        xe = x + 8
        lam, mu = lm[0, x + 4], lm[1, x + 4]
        e = all_strain(ext, xe, 8, NY, coefs)
        for slot in range(6):
            strain[slot, x] = e[slot]
        pressure = lam * (0.5 * (e[0] + e[3] + e[5]))
        sx[0, x + 4] = pressure + mu * e[0]
        shear = mu * e[1]
        sx[1, x + 4] = shear
        sy[0, x, 8 : 8 + NY, :] = shear
        shear = mu * e[2]
        sx[2, x + 4] = shear
        div[0, x] = deriv_z(shear, coefs)
        sy[1, x, 8 : 8 + NY, :] = pressure + mu * e[3]
        shear = mu * e[4]
        sy[2, x, 8 : 8 + NY, :] = shear
        div[1, x] = deriv_z(shear, coefs)
        div[2, x] = deriv_z(pressure + mu * e[5], coefs)
        for side, y0 in ((0, 4), (1, 8 + NY)):
            both = lmy[side, x]
            lam4, mu4 = both[:4], both[4:]
            g00 = deriv_x(ext, 0, xe, y0, 4)
            g11 = deriv_y(ext, 1, xe, y0, 4)
            g22 = deriv_z(ext[2, xe, y0 : y0 + 4, :], coefs)
            sy[0, x, y0 : y0 + 4, :] = mu4 * (
                deriv_x(ext, 1, xe, y0, 4) + deriv_y(ext, 0, xe, y0, 4)
            )
            sy[1, x, y0 : y0 + 4, :] = lam4 * (g00 + g11 + g22) + mu4 * (g11 + g11)
            sy[2, x, y0 : y0 + 4, :] = mu4 * (
                deriv_y(ext, 2, xe, y0, 4) + deriv_z(ext[1, xe, y0 : y0 + 4, :], coefs)
            )
        return carry

    lax.fori_loop(0, NX, plane, 0)

    def close(x, carry):
        for c in range(3):
            div[c, x] = div[c, x] + (
                deriv_x(sx, c, x + 4, 0, NY) + deriv_y(sy, c, x, 8, NY)
            )
        return carry

    lax.fori_loop(0, NX, close, 0)


def locate(cell):
    plane = lax.axis_size("gy") * NY * NZ
    ix = lax.div(cell, plane) - lax.axis_index("gx") * NX
    iy = lax.rem(lax.div(cell, NZ), lax.axis_size("gy") * NY) - lax.axis_index("gy") * NY
    iz = lax.rem(cell, NZ)
    inside = (ix >= 0) & (ix < NX) & (iy >= 0) & (iy < NY)
    return ix, iy, iz, inside


def add_force(div, c, ix, iy, iz, amount):
    lane = lax.broadcasted_iota(jnp.int32, (1, NZ), 1)
    row = div[c, ix, pl.ds(iy, 1), :]
    div[c, ix, pl.ds(iy, 1), :] = row + jnp.where(lane == iz, amount, 0.0)


def add_source(div, station, wavelet, start, offset):
    ix, iy, iz, inside = locate(station[0])

    @pl.when(inside)
    def _():
        add_force(div, 2, ix, iy, iz, wavelet[0, start[0] + offset])


def add_receivers(div, cells, counts, traces, start, offset):
    moment = start[0] + offset
    time = lax.broadcasted_iota(jnp.int32, traces.shape[2:], 1)

    def one(r, carry):
        ix, iy, iz, inside = locate(cells[0, r])

        @pl.when(inside)
        def _():
            amounts = jnp.sum(
                jnp.where(time == moment, traces[0, r], 0.0), axis=1, keepdims=True
            )
            for c in range(3):
                add_force(div, c, ix, iy, iz, amounts[c : c + 1])

        return carry

    lax.fori_loop(0, counts[0], one, 0)


def advance(now, old, div, rho, out, dot_with, dotted):
    def plane(x, carry):
        inverse = 1.0 / rho[x]
        summed = None
        for c in range(3):
            accel = div[c, x] * inverse
            if out is not None:
                out[c, x] = (2.0 * now[c, x] - old[c, x]) + (STEP_DT * STEP_DT) * accel
            if dotted is not None:
                term = dot_with[c, x] * accel
                summed = term if summed is None else summed + term
        if dotted is not None:
            dotted(x, summed)
        return carry

    lax.fori_loop(0, NX, plane, 0)


FIELD_SCRATCH = (
    pltpu.VMEM((3, NX + 16, NY + 16, NZ), F32),
    pltpu.VMEM((2, NX + 8, NY, NZ), F32),
    pltpu.VMEM((2, NX, 8, NZ), F32),
    pltpu.VMEM((3, NX + 8, NY, NZ), F32),
    pltpu.VMEM((3, NX, NY + 16, NZ), F32),
    pltpu.VMEM((3, NX, NY, NZ), F32),
)


def first_s(
    start, station, wavelet, s, bulk_e, bulk_o, rows_e, rows_o, par_e, par_o, vp, vs, rho, old, a,
    s1, strain, k_rho, send_e, send_o, ext, lm, lmy, sx, sy, div,
):
    fill_field(ext, s, (bulk_e, bulk_o), (rows_e, rows_o), 0, (par_e, par_o), 0)
    fill_lame(lm, lmy, vp, vs, rho, (rows_e, rows_o), (par_e, par_o))
    divergence(ext, lm, lmy, sx, sy, div, strain)
    add_source(div, station, wavelet, start, 1)

    def keep(x, value):
        k_rho[x] = value

    advance(s, old, div, rho, s1, a, keep)
    edge_rows(s1, send_e, send_o, 0)


def first_a(
    start, cells, counts, traces, a, bulk_e, bulk_o, rows_e, rows_o, par_e, par_o, vp, vs, rho, old,
    strain_s, a1, k_two, send_e, send_o, edge_e, edge_o, ext, lm, lmy, sx, sy, div, strain,
):
    fill_field(ext, a, (bulk_e, bulk_o), (rows_e, rows_o), 3 * NX, (par_e, par_o), 8)
    fill_lame(lm, lmy, vp, vs, rho, (rows_e, rows_o), (par_e, par_o))
    divergence(ext, lm, lmy, sx, sy, div, strain)
    add_receivers(div, cells, counts, traces, start, 1)
    advance(a, old, div, rho, a1, None, None)
    edge_rows(a1, send_e, send_o, 0)
    right = even("gx")
    for c in range(3):
        for i in range(4):
            high, low = a1[c, NX - 4 + i], a1[c, i]
            edge_e[c, i] = jnp.where(right, high, low)
            edge_o[c, i] = jnp.where(right, low, high)

    def products(x, carry):
        e_a = [strain[slot, x] for slot in range(6)]
        e_s = [strain_s[slot, x] for slot in range(6)]
        lam, mu = correlate(e_a, e_s)
        k_two[0, x] = lam
        k_two[1, x] = mu
        return carry

    lax.fori_loop(0, NX, products, 0)


def correlate(e_a, e_s):
    trace_a = e_a[0] + e_a[3] + e_a[5]
    trace_s = e_s[0] + e_s[3] + e_s[5]
    mu = 0.5 * (e_a[0] * e_s[0] + e_a[3] * e_s[3] + e_a[5] * e_s[5])
    mu = mu + (e_a[1] * e_s[1] + e_a[2] * e_s[2] + e_a[4] * e_s[4])
    return 0.25 * (trace_a * trace_s), mu


def second_s(
    start, station, wavelet, s, bulk_e, bulk_o, rows_e, rows_o, got_e, got_o, corner_e, corner_o,
    par_e, par_o, vp, vs, rho, a, k_rho_first, strain, k_rho, ext, lm, lmy, sx, sy, div,
):
    fill_field(ext, s, (bulk_e, bulk_o), (got_e, got_o), 0, (corner_e, corner_o), 0)
    fill_lame(lm, lmy, vp, vs, rho, (rows_e, rows_o), (par_e, par_o))
    divergence(ext, lm, lmy, sx, sy, div, strain)
    add_source(div, station, wavelet, start, 0)

    def keep(x, value):
        k_rho[x] = k_rho_first[x] + value

    advance(s, None, div, rho, None, a, keep)


def second_a(parts, a, edge_e, edge_o, got_e, got_o, vp, vs, rho, strain_s, k_two, k_rho, *rest):
    outs, (ext, kernels) = rest[:parts], rest[parts:]
    coefs = z_coefs()
    ext[:, 4 : 4 + NX, 8 : 8 + NY, :] = a[...]

    def put_x(left, right):
        ext[:, 0:4, 8 : 8 + NY, :] = left[...]
        ext[:, 4 + NX : 8 + NX, 8 : 8 + NY, :] = right[...]

    ordered("gx", edge_e, edge_o, put_x)

    def put_rows(below, above):
        for c in range(3):
            for x in range(NX):
                ext[c, 4 + x, 0:8, :] = below[c * NX + x]
                ext[c, 4 + x, 8 + NY : 16 + NY, :] = above[c * NX + x]

    ordered("gy", got_e, got_o, put_rows)

    def plane(x, carry):
        e_a = all_strain(ext, x + 4, 8, NY, coefs)
        lam, mu = correlate(e_a, [strain_s[slot, x] for slot in range(6)])
        lam = STEP_DT * (k_two[0, x] + lam)
        mu = STEP_DT * (k_two[1, x] + mu)
        density = rho[x]
        square_p, square_s = vp[x] * vp[x], vs[x] * vs[x]
        kernels[0, x] = 2.0 * density * square_p * lam
        kernels[1, x] = 2.0 * density * square_s * (mu - 2.0 * lam)
        kernels[2, x] = density * (
            STEP_DT * k_rho[x] + (square_p - 2.0 * square_s) * lam + square_s * mu
        )
        return carry

    lax.fori_loop(0, NX, plane, 0)
    share = NZ // parts
    lane = lax.broadcasted_iota(jnp.int32, (NY, NZ), 1)
    me = lax.axis_index("ens")
    for k in range(parts):
        first = share * jnp.bitwise_xor(me, k)

        def group(i, carry):
            kind, g = lax.div(i, NX // parts), lax.rem(i, NX // parts)
            packed = None
            for j in range(parts):
                shift = lax.rem(share * j - first + NZ, NZ)
                moved = pltpu.roll(kernels[kind, g * parts + j], shift, 1)
                packed = moved if packed is None else jnp.where(lane < share * j, packed, moved)
            outs[k][kind, g] = packed
            return carry

        lax.fori_loop(0, 3 * (NX // parts), group, 0)


def finish(parts, *refs):
    got, outs = refs[:parts], refs[parts:]
    share = NZ // parts
    for kind in range(3):
        for g in range(NX // parts):
            summed = got[0][kind, g]
            for k in range(1, parts):
                summed = summed + got[k][kind, g]
            for j in range(parts):
                moved = summed if j == 0 else pltpu.roll(summed, NZ - share * j, 1)
                outs[kind][g * parts + j] = moved[:, :share]


def swap(value, axis, odd):
    count = lax.axis_size(axis)
    pairs = [(i, i + 1) for i in range(odd, count - 1, 2)]
    return lax.ppermute(value, axis, pairs + [(j, i) for i, j in pairs])


def on_device(
    forward_now, forward_next, adjoint_now, adjoint_prev, speed_p, speed_s, density,
    station_cells, wavelets, receiver_cells, receiver_counts, adjoint_traces, start_step,
):
    s, old_s = forward_now[0], forward_next[0]
    a, old_a = adjoint_now[0], adjoint_prev[0]
    model = (speed_p, speed_s, density)
    start = start_step.reshape(1)
    work = 10_000_000
    s_e, s_o = swap(s, "gx", 0), swap(s, "gx", 1)
    rows = call(pack_y, (shapes(7 * NX, 8, NZ),) * 2, count=5, flops=work)(s, a, *model)
    rows_e, rows_o = swap(rows[0], "gy", 0), swap(rows[1], "gy", 1)
    par = call(pack_x, (shapes(48, 8, NZ),) * 2, count=5, flops=work)(rows_e, rows_o, *model)
    par_e, par_o = swap(par[0], "gx", 0), swap(par[1], "gx", 1)
    a_e, a_o = swap(a, "gx", 0), swap(a, "gx", 1)
    tile = shapes(3, NX, NY, NZ)
    strip = shapes(3 * NX, 8, NZ)
    s1, strain_s, k_rho, s1_rows_e, s1_rows_o = call(
        first_s, (tile, shapes(6, NX, NY, NZ), shapes(NX, NY, NZ), strip, strip),
        FIELD_SCRATCH, (0, 1, 2), 15, 10 * work,
    )(start, station_cells, wavelets, s, s_e, s_o, rows_e, rows_o, par_e, par_o, *model, old_s, a)
    s1_e, s1_o = swap(s1, "gx", 0), swap(s1, "gx", 1)
    s1_got_e, s1_got_o = swap(s1_rows_e, "gy", 0), swap(s1_rows_o, "gy", 1)
    corner = call(pack_corner, (shapes(8, 8, NZ),) * 2, count=2, flops=work)(s1_got_e, s1_got_o)
    corner_e, corner_o = swap(corner[0], "gx", 0), swap(corner[1], "gx", 1)
    edge = shapes(3, 4, NY, NZ)
    a1, k_two, a1_rows_e, a1_rows_o, a1_edge_e, a1_edge_o = call(
        first_a, (tile, shapes(2, NX, NY, NZ), strip, strip, edge, edge),
        FIELD_SCRATCH + (pltpu.VMEM((6, NX, NY, NZ), F32),), (0, 1, 2), 16, 10 * work,
    )(start, receiver_cells, receiver_counts, adjoint_traces, a, a_e, a_o, rows_e, rows_o,
      par_e, par_o, *model, old_a, strain_s)
    a1_e, a1_o = swap(a1_edge_e, "gx", 0), swap(a1_edge_o, "gx", 1)
    a1_got_e, a1_got_o = swap(a1_rows_e, "gy", 0), swap(a1_rows_o, "gy", 1)
    strain_s1, k_rho = call(
        second_s, (shapes(6, NX, NY, NZ), shapes(NX, NY, NZ)),
        FIELD_SCRATCH, (0, 1, 2), 19, 10 * work,
    )(start, station_cells, wavelets, s1, s1_e, s1_o, rows_e, rows_o, s1_got_e, s1_got_o,
      corner_e, corner_o, par_e, par_o, *model, a1, k_rho)
    parts = lax.axis_size("ens")
    pieces = call(
        functools.partial(second_a, parts), (shapes(3, NX // parts, NY, NZ),) * parts,
        (pltpu.VMEM((3, NX + 8, NY + 16, NZ), F32), pltpu.VMEM((3, NX, NY, NZ), F32)),
        (), 11, 10 * work,
    )(a1, a1_e, a1_o, a1_got_e, a1_got_o, *model, strain_s1, k_two, k_rho)
    got = [pieces[0]]
    for k in range(1, parts):
        got.append(lax.ppermute(pieces[k], "ens", [(i, i ^ k) for i in range(parts)]))
    return tuple(
        call(functools.partial(finish, parts), (shapes(NX, NY, NZ // parts),) * 3,
             count=parts, flops=work)(*got)
    )


def solution(mesh):
    return jax.shard_map(
        on_device,
        mesh=mesh,
        in_specs=(
            P("ens", None, "gx", "gy", None),
            P("ens", None, "gx", "gy", None),
            P("ens", None, "gx", "gy", None),
            P("ens", None, "gx", "gy", None),
            P("gx", "gy", None),
            P("gx", "gy", None),
            P("gx", "gy", None),
            P("ens"),
            P("ens", None),
            P("ens", None),
            P("ens"),
            P("ens", None, None, None),
            P(),
        ),
        out_specs=(P("gx", "gy", "ens"), P("gx", "gy", "ens"), P("gx", "gy", "ens")),
        check_vma=False,
    )
```

```python
import functools

import jax
import jax.numpy as jnp
from jax import lax
from jax.experimental import pallas as pl
from jax.experimental.pallas import tpu as pltpu
from jax.sharding import PartitionSpec as P

COEF = (0.8, -0.2, 4.0 / 105.0, -1.0 / 280.0)
STEP_DT = 0.25
F32 = jnp.float32
PAIRS = ((0, 0), (0, 1), (0, 2), (1, 1), (1, 2), (2, 2))
SLOT = {(0, 0): 0, (0, 1): 1, (0, 2): 2, (1, 0): 1, (1, 1): 3, (1, 2): 4, (2, 0): 2, (2, 1): 4, (2, 2): 5}
NX, NY, NZ = 8, 32, 128


def shapes(*dims):
    return jax.ShapeDtypeStruct(dims, F32)


def call(body, out_shape, *args, scratch=(), smem=(), hbm=(), vmem=40, flops=10_000_000):
    specs = [pl.BlockSpec(memory_space=pltpu.VMEM) for _ in args]
    for i in smem:
        specs[i] = pl.BlockSpec(memory_space=pltpu.SMEM)
    for i in hbm:
        specs[i] = pl.BlockSpec(memory_space=pltpu.HBM)
    return pl.pallas_call(
        body,
        out_shape=out_shape,
        in_specs=specs,
        out_specs=jax.tree.map(lambda _: pl.BlockSpec(memory_space=pltpu.VMEM), out_shape),
        scratch_shapes=list(scratch),
        compiler_params=pltpu.CompilerParams(vmem_limit_bytes=vmem << 20),
        cost_estimate=pl.CostEstimate(flops=flops, bytes_accessed=1 << 20, transcendentals=0),
    )(*args)


def even(axis):
    return lax.rem(lax.axis_index(axis), 2) == 0


def band():
    step = lax.broadcasted_iota(jnp.int32, (NZ, NZ), 0) - lax.broadcasted_iota(jnp.int32, (NZ, NZ), 1)
    matrix = jnp.zeros((NZ, NZ), F32)
    for k, value in zip(range(1, 5), (672.0, -168.0, 32.0, -3.0)):
        matrix = matrix + jnp.where(step == k, value, 0.0) - jnp.where(step == -k, value, 0.0)
    return jnp.concatenate([matrix.astype(jnp.bfloat16)] * 3, axis=0)


def deriv_z(value, matrix):
    flat = value.reshape(-1, NZ)
    high = flat.astype(jnp.bfloat16)
    rest = flat - high.astype(F32)
    middle = rest.astype(jnp.bfloat16)
    low = (rest - middle.astype(F32)).astype(jnp.bfloat16)
    terms = jnp.concatenate([high, middle, low], axis=1)
    return (jnp.dot(terms, matrix, preferred_element_type=F32) * (1.0 / 840.0)).reshape(value.shape)


def deriv_x(ref, c, x, y0, rows):
    summed = None
    for k in range(1, 5):
        term = COEF[k - 1] * (ref[c, x + k, pl.ds(y0, rows), :] - ref[c, x - k, pl.ds(y0, rows), :])
        summed = term if summed is None else summed + term
    return summed


def deriv_y(ref, c, x, y0, rows):
    summed = None
    for k in range(1, 5):
        term = COEF[k - 1] * (ref[c, x, pl.ds(y0 + k, rows), :] - ref[c, x, pl.ds(y0 - k, rows), :])
        summed = term if summed is None else summed + term
    return summed


def lame(vp, vs, rho):
    square_s = vs * vs
    return rho * (vp * vp - 2.0 * square_s), rho * square_s


def ordered(axis, got_even, got_odd, put):
    @pl.when(even(axis))
    def _():
        put(got_odd, got_even)

    @pl.when(jnp.logical_not(even(axis)))
    def _():
        put(got_even, got_odd)


def edge_rows(tile, out_e, out_o, base):
    upper = even("gy")
    for c in range(3):
        for x in range(NX):
            high, low = tile[c, x, NY - 8 :, :], tile[c, x, :8, :]
            out_e[base + c * NX + x] = jnp.where(upper, high, low)
            out_o[base + c * NX + x] = jnp.where(upper, low, high)


def pack_y(s, a, vp, vs, rho, out_e, out_o, model, sems):
    upper = even("gy")
    start = jnp.where(upper, NY - 8, 0)
    copies = []

    def begin(src, dst):
        copies.append(pltpu.make_async_copy(src, dst, sems.at[len(copies)]))
        copies[-1].start()

    for out, first in ((out_e, start), (out_o, NY - 8 - start)):
        rows = pl.ds(pl.multiple_of(first, 8), 8)
        for f, field in enumerate((s, a)):
            for c in range(3):
                at = (f * 3 + c) * NX
                begin(field.at[c, :, rows, :], out.at[at : at + NX])
        for i, field in enumerate((vp, vs, rho)):
            begin(field.at[:, rows, :], model.at[0 if out is out_e else 1, i])
    for copy in copies:
        copy.wait()
    for x in range(NX):
        for side, out in ((0, out_e), (1, out_o)):
            lam, mu = lame(model[side, 0, x], model[side, 1, x], model[side, 2, x])
            high = jnp.concatenate([lam[4:], mu[4:]], axis=0)
            low = jnp.concatenate([lam[:4], mu[:4]], axis=0)
            out[6 * NX + x] = jnp.where(upper if side == 0 else jnp.logical_not(upper), high, low)


def pack_corner_rows(got_e, got_o, out_e, out_o, fields):
    def put(below, above):
        right = even("gx")
        for f in range(fields):
            for c in range(2):
                for i in range(4):
                    row = [None, None]
                    for side, x in ((0, i), (1, NX - 4 + i)):
                        at = (f * 3 + c) * NX + x
                        row[side] = jnp.concatenate([below[at][4:], above[at][:4]], axis=0)
                    slot = (f * 2 + c) * 4 + i
                    out_e[slot] = jnp.where(right, row[1], row[0])
                    out_o[slot] = jnp.where(right, row[0], row[1])

    ordered("gy", got_e, got_o, put)


def pack_x(got_e, got_o, vp, vs, rho, out_e, out_o):
    pack_corner_rows(got_e, got_o, out_e, out_o, 2)
    right = even("gx")
    for i in range(4):
        low = lame(vp[i], vs[i], rho[i])
        high = lame(vp[NX - 4 + i], vs[NX - 4 + i], rho[NX - 4 + i])
        for which in range(2):
            for part in range(4):
                rows = slice(8 * part, 8 * part + 8)
                slot = 16 + (which * 4 + i) * 4 + part
                out_e[slot] = jnp.where(right, high[which][rows], low[which][rows])
                out_o[slot] = jnp.where(right, low[which][rows], high[which][rows])


RIM = 3 * NX
FOUR = RIM + 8


def pack_second(s1, a1, bulk_e, bulk_o, out_e, out_o):
    edge_rows(s1, out_e, out_o, 0)
    upper = even("gy")

    def put(left, right):
        for c in range(2):
            for i in range(4):
                before, after = left[c, NX - 4 + i], right[c, i]
                high = jnp.concatenate([before[NY - 4 :], after[NY - 4 :]], axis=0)
                low = jnp.concatenate([before[:4], after[:4]], axis=0)
                out_e[RIM + c * 4 + i] = jnp.where(upper, high, low)
                out_o[RIM + c * 4 + i] = jnp.where(upper, low, high)

    ordered("gx", bulk_e, bulk_o, put)
    for c in range(3):
        for i in range(4):
            high = jnp.concatenate([a1[c, i, NY - 4 :, :], a1[c, i + 4, NY - 4 :, :]], axis=0)
            low = jnp.concatenate([a1[c, i, :4, :], a1[c, i + 4, :4, :]], axis=0)
            out_e[FOUR + c * 4 + i] = jnp.where(upper, high, low)
            out_o[FOUR + c * 4 + i] = jnp.where(upper, low, high)


def fill_field(ext, tile, bulk, rows, base):
    ext[:, 8 : 8 + NX, 8 : 8 + NY, :] = tile[...]

    def put_x(left, right):
        ext[:, 0:8, 8 : 8 + NY, :] = left[...]
        ext[:, 8 + NX : 16 + NX, 8 : 8 + NY, :] = right[...]

    ordered("gx", bulk[0], bulk[1], put_x)

    def put_rows(below, above):
        for c in range(3):
            for x in range(NX):
                ext[c, 8 + x, 0:8, :] = below[base + c * NX + x]
                ext[c, 8 + x, 8 + NY : 16 + NY, :] = above[base + c * NX + x]

    ordered("gy", rows[0], rows[1], put_rows)


def fill_corner(ext, got, base):
    def put(left, right):
        for c in range(2):
            for i in range(4):
                at = base + c * 4 + i
                ext[c, 4 + i, 4:8, :] = left[at][:4]
                ext[c, 4 + i, 8 + NY : 12 + NY, :] = left[at][4:]
                ext[c, 8 + NX + i, 4:8, :] = right[at][:4]
                ext[c, 8 + NX + i, 8 + NY : 12 + NY, :] = right[at][4:]

    ordered("gx", got[0], got[1], put)


def fill_rim(ext, rows):
    def put(below, above):
        for c in range(2):
            for i in range(4):
                at = RIM + c * 4 + i
                ext[c, 4 + i, 4:8, :] = below[at][:4]
                ext[c, 8 + NX + i, 4:8, :] = below[at][4:]
                ext[c, 4 + i, 8 + NY : 12 + NY, :] = above[at][:4]
                ext[c, 8 + NX + i, 8 + NY : 12 + NY, :] = above[at][4:]

    ordered("gy", rows[0], rows[1], put)


def fill_lame(lm, lmy, vp, vs, rho, planes, rows):
    for x in range(NX):
        lam, mu = lame(vp[x], vs[x], rho[x])
        lm[0, 4 + x] = lam
        lm[1, 4 + x] = mu

    def put_x(left, right):
        for which in range(2):
            for i in range(4):
                for part in range(4):
                    at = 16 + (which * 4 + i) * 4 + part
                    lm[which, i, 8 * part : 8 * part + 8, :] = left[at]
                    lm[which, 4 + NX + i, 8 * part : 8 * part + 8, :] = right[at]

    ordered("gx", planes[0], planes[1], put_x)

    def put_rows(below, above):
        lmy[0] = below[6 * NX : 7 * NX]
        lmy[1] = above[6 * NX : 7 * NX]

    ordered("gy", rows[0], rows[1], put_rows)


def all_strain(ext, x, gz):
    g = [[None] * 3 for _ in range(3)]
    for j in range(3):
        g[0][j] = deriv_x(ext, j, x, 8, NY)
        g[1][j] = deriv_y(ext, j, x, 8, NY)
        g[2][j] = gz[j]
    return [g[i][j] + g[j][i] for i, j in PAIRS]


def divergence(ext, lm, lmy, sx, sy, div, strain, gz, gz_x, gz_y):
    matrix = band()
    for c in range(3):
        gz[c] = deriv_z(ext[c, 8 : 8 + NX, 8 : 8 + NY, :], matrix)
    for slot, c in enumerate((0, 2)):
        planes = [ext[c, 4:8, 8 : 8 + NY, :], ext[c, 8 + NX : 12 + NX, 8 : 8 + NY, :]]
        gz_x[slot] = deriv_z(jnp.concatenate(planes, axis=0), matrix)
    for slot, c in enumerate((1, 2)):
        rows = [ext[c, 8 : 8 + NX, 4:8, :], ext[c, 8 : 8 + NX, 8 + NY : 12 + NY, :]]
        gz_y[slot] = deriv_z(jnp.concatenate(rows, axis=1), matrix)

    def halo_plane(i, carry):
        x = jnp.where(i < 4, i, i + NX)
        xe = x + 4
        lam, mu = lm[0, x], lm[1, x]
        g00 = deriv_x(ext, 0, xe, 8, NY)
        g11 = deriv_y(ext, 1, xe, 8, NY)
        sx[0, x] = lam * (g00 + g11 + gz_x[1, i]) + mu * (g00 + g00)
        sx[1, x] = mu * (deriv_x(ext, 1, xe, 8, NY) + deriv_y(ext, 0, xe, 8, NY))
        sx[2, x] = mu * (deriv_x(ext, 2, xe, 8, NY) + gz_x[0, i])
        return carry

    lax.fori_loop(0, 8, halo_plane, 0)

    def plane(x, carry):
        xe = x + 8
        lam, mu = lm[0, x + 4], lm[1, x + 4]
        e = all_strain(ext, xe, [gz[j, x] for j in range(3)])
        for slot in range(6):
            strain[slot, x] = e[slot]
        pressure = lam * (0.5 * (e[0] + e[3] + e[5]))
        sx[0, x + 4] = pressure + mu * e[0]
        shear = mu * e[1]
        sx[1, x + 4] = shear
        sy[0, x, 8 : 8 + NY, :] = shear
        shear = mu * e[2]
        sx[2, x + 4] = shear
        gz[0, x] = shear
        sy[1, x, 8 : 8 + NY, :] = pressure + mu * e[3]
        shear = mu * e[4]
        sy[2, x, 8 : 8 + NY, :] = shear
        gz[1, x] = shear
        gz[2, x] = pressure + mu * e[5]
        for side, y0 in ((0, 4), (1, 8 + NY)):
            both = lmy[side, x]
            lam4, mu4 = both[:4], both[4:]
            g00 = deriv_x(ext, 0, xe, y0, 4)
            g11 = deriv_y(ext, 1, xe, y0, 4)
            rows = slice(4 * side, 4 * side + 4)
            sy[0, x, y0 : y0 + 4, :] = mu4 * (
                deriv_x(ext, 1, xe, y0, 4) + deriv_y(ext, 0, xe, y0, 4)
            )
            sy[1, x, y0 : y0 + 4, :] = lam4 * (g00 + g11 + gz_y[1, x, rows, :]) + mu4 * (g11 + g11)
            sy[2, x, y0 : y0 + 4, :] = mu4 * (
                deriv_y(ext, 2, xe, y0, 4) + gz_y[0, x, rows, :]
            )
        return carry

    lax.fori_loop(0, NX, plane, 0)
    for c in range(3):
        div[c] = deriv_z(gz[c], matrix)

    def close(x, carry):
        for c in range(3):
            div[c, x] = div[c, x] + (
                deriv_x(sx, c, x + 4, 0, NY) + deriv_y(sy, c, x, 8, NY)
            )
        return carry

    lax.fori_loop(0, NX, close, 0)


def locate(cell):
    plane = lax.axis_size("gy") * NY * NZ
    ix = lax.div(cell, plane) - lax.axis_index("gx") * NX
    iy = lax.rem(lax.div(cell, NZ), lax.axis_size("gy") * NY) - lax.axis_index("gy") * NY
    iz = lax.rem(cell, NZ)
    inside = (ix >= 0) & (ix < NX) & (iy >= 0) & (iy < NY)
    return ix, iy, iz, inside


def add_force(div, c, ix, iy, iz, amount):
    lane = lax.broadcasted_iota(jnp.int32, (1, NZ), 1)
    row = div[c, ix, pl.ds(iy, 1), :]
    div[c, ix, pl.ds(iy, 1), :] = row + jnp.where(lane == iz, amount, 0.0)


def add_source(div, station, wavelet, start, offset):
    ix, iy, iz, inside = locate(station[0])

    @pl.when(inside)
    def _():
        add_force(div, 2, ix, iy, iz, wavelet[0, start[0] + offset])


def add_receivers(div, cells, counts, traces, start, offset):
    moment = start[0] + offset
    time = lax.broadcasted_iota(jnp.int32, (3, traces.shape[2]), 1)

    def one(r, carry):
        ix, iy, iz, inside = locate(cells[0, r])

        @pl.when(inside)
        def _():
            amounts = jnp.sum(
                jnp.where(time == moment, traces[:, r, :], 0.0), axis=1, keepdims=True
            )
            for c in range(3):
                add_force(div, c, ix, iy, iz, amounts[c : c + 1])

        return carry

    lax.fori_loop(0, counts[0], one, 0)


def advance(now, old, div, rho, out, dot_with, dotted):
    def plane(x, carry):
        inverse = 1.0 / rho[x]
        summed = None
        for c in range(3):
            accel = div[c, x] * inverse
            if out is not None:
                out[c, x] = (2.0 * now[c, x] - old[c, x]) + (STEP_DT * STEP_DT) * accel
            if dotted is not None:
                term = dot_with[c, x] * accel
                summed = term if summed is None else summed + term
        if dotted is not None:
            dotted(x, summed)
        return carry

    lax.fori_loop(0, NX, plane, 0)


FIELD_SCRATCH = (
    pltpu.VMEM((3, NX + 16, NY + 16, NZ), F32),
    pltpu.VMEM((2, NX + 8, NY, NZ), F32),
    pltpu.VMEM((2, NX, 8, NZ), F32),
    pltpu.VMEM((3, NX + 8, NY, NZ), F32),
    pltpu.VMEM((3, NX, NY + 16, NZ), F32),
    pltpu.VMEM((3, NX, NY, NZ), F32),
    pltpu.VMEM((3, NX, NY, NZ), F32),
    pltpu.VMEM((2, 8, NY, NZ), F32),
    pltpu.VMEM((2, NX, 8, NZ), F32),
)


def first_s(
    start, station, wavelet, s, bulk_e, bulk_o, rows_e, rows_o, par_e, par_o,
    vp, vs, rho, old, a, s1, strain, k_rho, ext, lm, lmy, sx, sy, div, *depth,
):
    fill_field(ext, s, (bulk_e, bulk_o), (rows_e, rows_o), 0)
    fill_corner(ext, (par_e, par_o), 0)
    fill_lame(lm, lmy, vp, vs, rho, (par_e, par_o), (rows_e, rows_o))
    divergence(ext, lm, lmy, sx, sy, div, strain, *depth)
    add_source(div, station, wavelet, start, 1)

    def keep(x, value):
        k_rho[x] = value

    advance(s, old, div, rho, s1, a, keep)


def first_a(
    start, cells, counts, traces, a, bulk_e, bulk_o, rows_e, rows_o, par_e, par_o,
    vp, vs, rho, old, strain_s, a1, k_two, edge_e, edge_o,
    ext, lm, lmy, sx, sy, div, gz, gz_x, gz_y, strain,
):
    fill_field(ext, a, (bulk_e, bulk_o), (rows_e, rows_o), 3 * NX)
    fill_corner(ext, (par_e, par_o), 8)
    fill_lame(lm, lmy, vp, vs, rho, (par_e, par_o), (rows_e, rows_o))
    divergence(ext, lm, lmy, sx, sy, div, strain, gz, gz_x, gz_y)
    add_receivers(div, cells, counts, traces, start, 1)
    advance(a, old, div, rho, a1, None, None)
    right = even("gx")
    for c in range(3):
        for i in range(4):
            high, low = a1[c, NX - 4 + i], a1[c, i]
            edge_e[c, i] = jnp.where(right, high, low)
            edge_o[c, i] = jnp.where(right, low, high)

    def products(x, carry):
        e_a = [strain[slot, x] for slot in range(6)]
        e_s = [strain_s[slot, x] for slot in range(6)]
        lam, mu = correlate(e_a, e_s)
        k_two[0, x] = lam
        k_two[1, x] = mu
        return carry

    lax.fori_loop(0, NX, products, 0)


def correlate(e_a, e_s):
    trace_a = e_a[0] + e_a[3] + e_a[5]
    trace_s = e_s[0] + e_s[3] + e_s[5]
    mu = 0.5 * (e_a[0] * e_s[0] + e_a[3] * e_s[3] + e_a[5] * e_s[5])
    mu = mu + (e_a[1] * e_s[1] + e_a[2] * e_s[2] + e_a[4] * e_s[4])
    return 0.25 * (trace_a * trace_s), mu


def second_s(
    start, station, wavelet, s, bulk_e, bulk_o, rows_e, rows_o, first_e, first_o, par_e, par_o,
    vp, vs, rho, a, k_rho_first, strain, k_rho, ext, lm, lmy, sx, sy, div, *depth,
):
    fill_field(ext, s, (bulk_e, bulk_o), (rows_e, rows_o), 0)
    fill_rim(ext, (rows_e, rows_o))
    fill_lame(lm, lmy, vp, vs, rho, (par_e, par_o), (first_e, first_o))
    divergence(ext, lm, lmy, sx, sy, div, strain, *depth)
    add_source(div, station, wavelet, start, 0)

    def keep(x, value):
        k_rho[x] = k_rho_first[x] + value

    advance(s, None, div, rho, None, a, keep)


def second_a(parts, a, edge_e, edge_o, got_e, got_o, vp, vs, rho, strain_s, k_two, k_rho, *rest):
    outs, (ext, kernels) = rest[:parts], rest[parts:]
    matrix = band()
    ext[:, 4 : 4 + NX, 8 : 8 + NY, :] = a[...]

    def put_x(left, right):
        ext[:, 0:4, 8 : 8 + NY, :] = left[...]
        ext[:, 4 + NX : 8 + NX, 8 : 8 + NY, :] = right[...]

    ordered("gx", edge_e, edge_o, put_x)

    def put_rows(below, above):
        for c in range(3):
            for i in range(4):
                at = FOUR + c * 4 + i
                ext[c, 4 + i, 4:8, :] = below[at][:4]
                ext[c, 8 + i, 4:8, :] = below[at][4:]
                ext[c, 4 + i, 8 + NY : 12 + NY, :] = above[at][:4]
                ext[c, 8 + i, 8 + NY : 12 + NY, :] = above[at][4:]

    ordered("gy", got_e, got_o, put_rows)

    for c in range(3):
        kernels[c] = deriv_z(a[c], matrix)

    def plane(x, carry):
        e_a = all_strain(ext, x + 4, [kernels[j, x] for j in range(3)])
        lam, mu = correlate(e_a, [strain_s[slot, x] for slot in range(6)])
        lam = STEP_DT * (k_two[0, x] + lam)
        mu = STEP_DT * (k_two[1, x] + mu)
        density = rho[x]
        square_p, square_s = vp[x] * vp[x], vs[x] * vs[x]
        kernels[0, x] = 2.0 * density * square_p * lam
        kernels[1, x] = 2.0 * density * square_s * (mu - 2.0 * lam)
        kernels[2, x] = density * (
            STEP_DT * k_rho[x] + (square_p - 2.0 * square_s) * lam + square_s * mu
        )
        return carry

    lax.fori_loop(0, NX, plane, 0)
    share = NZ // parts
    lane = lax.broadcasted_iota(jnp.int32, (NY, NZ), 1)
    me = lax.axis_index("ens")
    for k in range(parts):
        first = share * jnp.bitwise_xor(me, k)

        def group(i, carry):
            kind, g = lax.div(i, NX // parts), lax.rem(i, NX // parts)
            packed = None
            for j in range(parts):
                shift = lax.rem(share * j - first + NZ, NZ)
                moved = pltpu.roll(kernels[kind, g * parts + j], shift, 1)
                packed = moved if packed is None else jnp.where(lane < share * j, packed, moved)
            outs[k][kind, g] = packed
            return carry

        lax.fori_loop(0, 3 * (NX // parts), group, 0)


def finish(parts, *refs):
    got, outs = refs[:parts], refs[parts:]
    share = NZ // parts
    for kind in range(3):
        for g in range(NX // parts):
            summed = got[0][kind, g]
            for k in range(1, parts):
                summed = summed + got[k][kind, g]
            for j in range(parts):
                moved = summed if j == 0 else pltpu.roll(summed, NZ - share * j, 1)
                outs[kind][g * parts + j] = moved[:, :share]


def swap(value, axis, odd):
    count = lax.axis_size(axis)
    pairs = [(i, i + 1) for i in range(odd, count - 1, 2)]
    return lax.ppermute(value, axis, pairs + [(j, i) for i, j in pairs])


def on_device(
    forward_now, forward_next, adjoint_now, adjoint_prev, speed_p, speed_s, density,
    station_cells, wavelets, receiver_cells, receiver_counts, adjoint_traces, start_step,
):
    s, old_s = forward_now[0], forward_next[0]
    a, old_a = adjoint_now[0], adjoint_prev[0]
    model = (speed_p, speed_s, density)
    start = start_step.reshape(1)
    work = 100_000_000
    tile = shapes(3, NX, NY, NZ)
    rows = call(
        pack_y, (shapes(7 * NX, 8, NZ),) * 2, s, a, *model,
        scratch=(pltpu.VMEM((2, 3, NX, 8, NZ), F32), pltpu.SemaphoreType.DMA((18,))),
        hbm=range(5), vmem=60,
    )
    rows = swap(rows[0], "gy", 0), swap(rows[1], "gy", 1)
    s_e, s_o = swap(s, "gx", 0), swap(s, "gx", 1)
    par = call(pack_x, (shapes(48, 8, NZ),) * 2, *rows, *model)
    a_sent = lax.optimization_barrier((a, par))[0]
    par = swap(par[0], "gx", 0), swap(par[1], "gx", 1)
    a_e, a_o = swap(a_sent, "gx", 0), swap(a_sent, "gx", 1)
    s1, strain_s, k_rho = call(
        first_s, (tile, shapes(6, NX, NY, NZ), shapes(NX, NY, NZ)),
        start, station_cells, wavelets, s, s_e, s_o, *rows, *par, *model, old_s, a,
        scratch=FIELD_SCRATCH, smem=(0, 1, 2), flops=work,
    )
    s1, a_e, a_o = lax.optimization_barrier((s1, a_e, a_o))
    s1_e, s1_o = swap(s1, "gx", 0), swap(s1, "gx", 1)
    edge = shapes(3, 4, NY, NZ)
    a1, k_two, edge_e, edge_o = call(
        first_a, (tile, shapes(2, NX, NY, NZ), edge, edge),
        start, receiver_cells, receiver_counts, adjoint_traces[0].transpose(1, 0, 2),
        a, a_e, a_o, *rows, *par, *model, old_a, strain_s,
        scratch=FIELD_SCRATCH + (pltpu.VMEM((6, NX, NY, NZ), F32),), smem=(0, 1, 2), flops=work,
    )
    a1_e, a1_o = swap(edge_e, "gx", 0), swap(edge_o, "gx", 1)
    rim = call(pack_second, (shapes(FOUR + 12, 8, NZ),) * 2, s1, a1, s1_e, s1_o)
    rim = swap(rim[0], "gy", 0), swap(rim[1], "gy", 1)
    strain_s1, k_rho = call(
        second_s, (shapes(6, NX, NY, NZ), shapes(NX, NY, NZ)),
        start, station_cells, wavelets, s1, s1_e, s1_o, *rim, *rows, *par, *model, a1, k_rho,
        scratch=FIELD_SCRATCH, smem=(0, 1, 2), flops=work,
    )
    parts = lax.axis_size("ens")
    pieces = call(
        functools.partial(second_a, parts), (shapes(3, NX // parts, NY, NZ),) * parts,
        a1, a1_e, a1_o, *rim, *model, strain_s1, k_two, k_rho,
        scratch=(pltpu.VMEM((3, NX + 8, NY + 16, NZ), F32), pltpu.VMEM((3, NX, NY, NZ), F32)),
        flops=work,
    )
    got = [pieces[0]]
    for k in range(1, parts):
        got.append(lax.ppermute(pieces[k], "ens", [(i, i ^ k) for i in range(parts)]))
    return tuple(
        call(functools.partial(finish, parts), (shapes(NX, NY, NZ // parts),) * 3, *got)
    )


def solution(mesh):
    return jax.shard_map(
        on_device,
        mesh=mesh,
        in_specs=(
            P("ens", None, "gx", "gy", None),
            P("ens", None, "gx", "gy", None),
            P("ens", None, "gx", "gy", None),
            P("ens", None, "gx", "gy", None),
            P("gx", "gy", None),
            P("gx", "gy", None),
            P("gx", "gy", None),
            P("ens"),
            P("ens", None),
            P("ens", None),
            P("ens"),
            P("ens", None, None, None),
            P(),
        ),
        out_specs=(P("gx", "gy", "ens"), P("gx", "gy", "ens"), P("gx", "gy", "ens")),
        check_vma=False,
    )
```

```python
import functools

import jax
import jax.numpy as jnp
from jax import lax
from jax.experimental import pallas as pl
from jax.experimental.pallas import tpu as pltpu
from jax.sharding import PartitionSpec as P

COEF = (0.8, -0.2, 4.0 / 105.0, -1.0 / 280.0)
STEP_DT = 0.25
F32 = jnp.float32
PAIRS = ((0, 0), (0, 1), (0, 2), (1, 1), (1, 2), (2, 2))
SLOT = {(0, 0): 0, (0, 1): 1, (0, 2): 2, (1, 0): 1, (1, 1): 3, (1, 2): 4, (2, 0): 2, (2, 1): 4, (2, 2): 5}
NX, NY, NZ = 8, 32, 128


def shapes(*dims):
    return jax.ShapeDtypeStruct(dims, F32)


def call(body, out_shape, *args, scratch=(), smem=(), hbm=(), vmem=40, flops=10_000_000):
    specs = [pl.BlockSpec(memory_space=pltpu.VMEM) for _ in args]
    for i in smem:
        specs[i] = pl.BlockSpec(memory_space=pltpu.SMEM)
    for i in hbm:
        specs[i] = pl.BlockSpec(memory_space=pltpu.HBM)
    return pl.pallas_call(
        body,
        out_shape=out_shape,
        in_specs=specs,
        out_specs=jax.tree.map(lambda _: pl.BlockSpec(memory_space=pltpu.VMEM), out_shape),
        scratch_shapes=list(scratch),
        compiler_params=pltpu.CompilerParams(vmem_limit_bytes=vmem << 20),
        cost_estimate=pl.CostEstimate(flops=flops, bytes_accessed=1 << 20, transcendentals=0),
    )(*args)


def even(axis):
    return lax.rem(lax.axis_index(axis), 2) == 0


def band():
    step = lax.broadcasted_iota(jnp.int32, (NZ, NZ), 0) - lax.broadcasted_iota(jnp.int32, (NZ, NZ), 1)
    matrix = jnp.zeros((NZ, NZ), F32)
    for k, value in zip(range(1, 5), (672.0, -168.0, 32.0, -3.0)):
        matrix = matrix + jnp.where(step == k, value, 0.0) - jnp.where(step == -k, value, 0.0)
    return jnp.concatenate([matrix.astype(jnp.bfloat16)] * 3, axis=0)


def deriv_z(value, matrix):
    flat = value.reshape(-1, NZ)
    high = flat.astype(jnp.bfloat16)
    rest = flat - high.astype(F32)
    middle = rest.astype(jnp.bfloat16)
    low = (rest - middle.astype(F32)).astype(jnp.bfloat16)
    terms = jnp.concatenate([high, middle, low], axis=1)
    return (jnp.dot(terms, matrix, preferred_element_type=F32) * (1.0 / 840.0)).reshape(value.shape)


def deriv_x(ref, c, x, y0, rows):
    summed = None
    for k in range(1, 5):
        term = COEF[k - 1] * (ref[c, x + k, pl.ds(y0, rows), :] - ref[c, x - k, pl.ds(y0, rows), :])
        summed = term if summed is None else summed + term
    return summed


def deriv_y(ref, c, x, y0, rows):
    summed = None
    for k in range(1, 5):
        term = COEF[k - 1] * (ref[c, x, pl.ds(y0 + k, rows), :] - ref[c, x, pl.ds(y0 - k, rows), :])
        summed = term if summed is None else summed + term
    return summed


def lame(vp, vs, rho):
    square_s = vs * vs
    return rho * (vp * vp - 2.0 * square_s), rho * square_s


def ordered(axis, got_even, got_odd, put):
    @pl.when(even(axis))
    def _():
        put(got_odd, got_even)

    @pl.when(jnp.logical_not(even(axis)))
    def _():
        put(got_even, got_odd)


def edge_rows(tile, out_e, out_o, base):
    upper = even("gy")
    for c in range(3):
        for x in range(NX):
            high, low = tile[c, x, NY - 8 :, :], tile[c, x, :8, :]
            out_e[base + c * NX + x] = jnp.where(upper, high, low)
            out_o[base + c * NX + x] = jnp.where(upper, low, high)


def pack_y(s, a, vp, vs, rho, out_e, out_o, model, sems):
    upper = even("gy")
    start = jnp.where(upper, NY - 8, 0)
    copies = []

    def begin(src, dst):
        copies.append(pltpu.make_async_copy(src, dst, sems.at[len(copies)]))
        copies[-1].start()

    for out, first in ((out_e, start), (out_o, NY - 8 - start)):
        rows = pl.ds(pl.multiple_of(first, 8), 8)
        for f, field in enumerate((s, a)):
            for c in range(3):
                at = (f * 3 + c) * NX
                begin(field.at[c, :, rows, :], out.at[at : at + NX])
        for i, field in enumerate((vp, vs, rho)):
            begin(field.at[:, rows, :], model.at[0 if out is out_e else 1, i])
    for copy in copies:
        copy.wait()
    for x in range(NX):
        for side, out in ((0, out_e), (1, out_o)):
            lam, mu = lame(model[side, 0, x], model[side, 1, x], model[side, 2, x])
            high = jnp.concatenate([lam[4:], mu[4:]], axis=0)
            low = jnp.concatenate([lam[:4], mu[:4]], axis=0)
            out[6 * NX + x] = jnp.where(upper if side == 0 else jnp.logical_not(upper), high, low)


def pack_corner_rows(got_e, got_o, out_e, out_o, fields):
    def put(below, above):
        right = even("gx")
        for f in range(fields):
            for c in range(2):
                for i in range(4):
                    row = [None, None]
                    for side, x in ((0, i), (1, NX - 4 + i)):
                        at = (f * 3 + c) * NX + x
                        row[side] = jnp.concatenate([below[at][4:], above[at][:4]], axis=0)
                    slot = (f * 2 + c) * 4 + i
                    out_e[slot] = jnp.where(right, row[1], row[0])
                    out_o[slot] = jnp.where(right, row[0], row[1])

    ordered("gy", got_e, got_o, put)


def pack_x(got_e, got_o, vp, vs, rho, station, wavelet, cells, counts, traces, out_e, out_o):
    pack_corner_rows(got_e, got_o, out_e, out_o, 2)
    right = even("gx")
    for i in range(4):
        low = lame(vp[i], vs[i], rho[i])
        high = lame(vp[NX - 4 + i], vs[NX - 4 + i], rho[NX - 4 + i])
        for which in range(2):
            for part in range(4):
                rows = slice(8 * part, 8 * part + 8)
                slot = 16 + (which * 4 + i) * 4 + part
                out_e[slot] = jnp.where(right, high[which][rows], low[which][rows])
                out_o[slot] = jnp.where(right, low[which][rows], high[which][rows])


RIM = 3 * NX
FOUR = RIM + 8


def pack_second(s1, a1, bulk_e, bulk_o, out_e, out_o):
    edge_rows(s1, out_e, out_o, 0)
    upper = even("gy")

    def put(left, right):
        for c in range(2):
            for i in range(4):
                before, after = left[c, NX - 4 + i], right[c, i]
                high = jnp.concatenate([before[NY - 4 :], after[NY - 4 :]], axis=0)
                low = jnp.concatenate([before[:4], after[:4]], axis=0)
                out_e[RIM + c * 4 + i] = jnp.where(upper, high, low)
                out_o[RIM + c * 4 + i] = jnp.where(upper, low, high)

    ordered("gx", bulk_e, bulk_o, put)
    for c in range(3):
        for i in range(4):
            high = jnp.concatenate([a1[c, i, NY - 4 :, :], a1[c, i + 4, NY - 4 :, :]], axis=0)
            low = jnp.concatenate([a1[c, i, :4, :], a1[c, i + 4, :4, :]], axis=0)
            out_e[FOUR + c * 4 + i] = jnp.where(upper, high, low)
            out_o[FOUR + c * 4 + i] = jnp.where(upper, low, high)


def fill_field(ext, tile, bulk, rows, base):
    ext[:, 8 : 8 + NX, 8 : 8 + NY, :] = tile[...]

    def put_x(left, right):
        ext[:, 0:8, 8 : 8 + NY, :] = left[...]
        ext[:, 8 + NX : 16 + NX, 8 : 8 + NY, :] = right[...]

    ordered("gx", bulk[0], bulk[1], put_x)

    def put_rows(below, above):
        for c in range(3):
            for x in range(NX):
                ext[c, 8 + x, 0:8, :] = below[base + c * NX + x]
                ext[c, 8 + x, 8 + NY : 16 + NY, :] = above[base + c * NX + x]

    ordered("gy", rows[0], rows[1], put_rows)


def fill_corner(ext, got, base):
    def put(left, right):
        for c in range(2):
            for i in range(4):
                at = base + c * 4 + i
                ext[c, 4 + i, 4:8, :] = left[at][:4]
                ext[c, 4 + i, 8 + NY : 12 + NY, :] = left[at][4:]
                ext[c, 8 + NX + i, 4:8, :] = right[at][:4]
                ext[c, 8 + NX + i, 8 + NY : 12 + NY, :] = right[at][4:]

    ordered("gx", got[0], got[1], put)


def fill_rim(ext, rows):
    def put(below, above):
        for c in range(2):
            for i in range(4):
                at = RIM + c * 4 + i
                ext[c, 4 + i, 4:8, :] = below[at][:4]
                ext[c, 8 + NX + i, 4:8, :] = below[at][4:]
                ext[c, 4 + i, 8 + NY : 12 + NY, :] = above[at][:4]
                ext[c, 8 + NX + i, 8 + NY : 12 + NY, :] = above[at][4:]

    ordered("gy", rows[0], rows[1], put)


def fill_lame(lm, lmy, vp, vs, rho, planes, rows):
    for x in range(NX):
        lam, mu = lame(vp[x], vs[x], rho[x])
        lm[0, 4 + x] = lam
        lm[1, 4 + x] = mu

    def put_x(left, right):
        for which in range(2):
            for i in range(4):
                for part in range(4):
                    at = 16 + (which * 4 + i) * 4 + part
                    lm[which, i, 8 * part : 8 * part + 8, :] = left[at]
                    lm[which, 4 + NX + i, 8 * part : 8 * part + 8, :] = right[at]

    ordered("gx", planes[0], planes[1], put_x)

    def put_rows(below, above):
        lmy[0] = below[6 * NX : 7 * NX]
        lmy[1] = above[6 * NX : 7 * NX]

    ordered("gy", rows[0], rows[1], put_rows)


def all_strain(ext, x, gz):
    g = [[None] * 3 for _ in range(3)]
    for j in range(3):
        g[0][j] = deriv_x(ext, j, x, 8, NY)
        g[1][j] = deriv_y(ext, j, x, 8, NY)
        g[2][j] = gz[j]
    return [g[i][j] + g[j][i] for i, j in PAIRS]


def divergence(ext, lm, lmy, sx, sy, div, strain, gz, gz_x, gz_y):
    matrix = band()
    for c in range(3):
        gz[c] = deriv_z(ext[c, 8 : 8 + NX, 8 : 8 + NY, :], matrix)
    for slot, c in enumerate((0, 2)):
        planes = [ext[c, 4:8, 8 : 8 + NY, :], ext[c, 8 + NX : 12 + NX, 8 : 8 + NY, :]]
        gz_x[slot] = deriv_z(jnp.concatenate(planes, axis=0), matrix)
    for slot, c in enumerate((1, 2)):
        rows = [ext[c, 8 : 8 + NX, 4:8, :], ext[c, 8 : 8 + NX, 8 + NY : 12 + NY, :]]
        gz_y[slot] = deriv_z(jnp.concatenate(rows, axis=1), matrix)

    def halo_plane(i, carry):
        x = jnp.where(i < 4, i, i + NX)
        xe = x + 4
        lam, mu = lm[0, x], lm[1, x]
        g00 = deriv_x(ext, 0, xe, 8, NY)
        g11 = deriv_y(ext, 1, xe, 8, NY)
        sx[0, x] = lam * (g00 + g11 + gz_x[1, i]) + mu * (g00 + g00)
        sx[1, x] = mu * (deriv_x(ext, 1, xe, 8, NY) + deriv_y(ext, 0, xe, 8, NY))
        sx[2, x] = mu * (deriv_x(ext, 2, xe, 8, NY) + gz_x[0, i])
        return carry

    lax.fori_loop(0, 8, halo_plane, 0)

    def plane(x, carry):
        xe = x + 8
        lam, mu = lm[0, x + 4], lm[1, x + 4]
        e = all_strain(ext, xe, [gz[j, x] for j in range(3)])
        for slot in range(6):
            strain[slot, x] = e[slot]
        pressure = lam * (0.5 * (e[0] + e[3] + e[5]))
        sx[0, x + 4] = pressure + mu * e[0]
        shear = mu * e[1]
        sx[1, x + 4] = shear
        sy[0, x, 8 : 8 + NY, :] = shear
        shear = mu * e[2]
        sx[2, x + 4] = shear
        gz[0, x] = shear
        sy[1, x, 8 : 8 + NY, :] = pressure + mu * e[3]
        shear = mu * e[4]
        sy[2, x, 8 : 8 + NY, :] = shear
        gz[1, x] = shear
        gz[2, x] = pressure + mu * e[5]
        for side, y0 in ((0, 4), (1, 8 + NY)):
            both = lmy[side, x]
            lam4, mu4 = both[:4], both[4:]
            g00 = deriv_x(ext, 0, xe, y0, 4)
            g11 = deriv_y(ext, 1, xe, y0, 4)
            rows = slice(4 * side, 4 * side + 4)
            sy[0, x, y0 : y0 + 4, :] = mu4 * (
                deriv_x(ext, 1, xe, y0, 4) + deriv_y(ext, 0, xe, y0, 4)
            )
            sy[1, x, y0 : y0 + 4, :] = lam4 * (g00 + g11 + gz_y[1, x, rows, :]) + mu4 * (g11 + g11)
            sy[2, x, y0 : y0 + 4, :] = mu4 * (
                deriv_y(ext, 2, xe, y0, 4) + gz_y[0, x, rows, :]
            )
        return carry

    lax.fori_loop(0, NX, plane, 0)
    for c in range(3):
        div[c] = deriv_z(gz[c], matrix)

    def close(x, carry):
        for c in range(3):
            div[c, x] = div[c, x] + (
                deriv_x(sx, c, x + 4, 0, NY) + deriv_y(sy, c, x, 8, NY)
            )
        return carry

    lax.fori_loop(0, NX, close, 0)


def locate(cell):
    plane = lax.axis_size("gy") * NY * NZ
    ix = lax.div(cell, plane) - lax.axis_index("gx") * NX
    iy = lax.rem(lax.div(cell, NZ), lax.axis_size("gy") * NY) - lax.axis_index("gy") * NY
    iz = lax.rem(cell, NZ)
    inside = (ix >= 0) & (ix < NX) & (iy >= 0) & (iy < NY)
    return ix, iy, iz, inside


def add_force(div, c, ix, iy, iz, amount):
    lane = lax.broadcasted_iota(jnp.int32, (1, NZ), 1)
    row = div[c, ix, pl.ds(iy, 1), :]
    div[c, ix, pl.ds(iy, 1), :] = row + jnp.where(lane == iz, amount, 0.0)


def add_source(div, station, wavelet, start, offset):
    ix, iy, iz, inside = locate(station[0])

    @pl.when(inside)
    def _():
        add_force(div, 2, ix, iy, iz, wavelet[0, start[0] + offset])


def add_receivers(div, cells, counts, traces, start, offset):
    moment = start[0] + offset
    time = lax.broadcasted_iota(jnp.int32, (3, traces.shape[2]), 1)

    def one(r, carry):
        ix, iy, iz, inside = locate(cells[0, r])

        @pl.when(inside)
        def _():
            amounts = jnp.sum(
                jnp.where(time == moment, traces[:, r, :], 0.0), axis=1, keepdims=True
            )
            for c in range(3):
                add_force(div, c, ix, iy, iz, amounts[c : c + 1])

        return carry

    lax.fori_loop(0, counts[0], one, 0)


def advance(now, old, div, rho, out, dot_with, dotted):
    def plane(x, carry):
        inverse = 1.0 / rho[x]
        summed = None
        for c in range(3):
            accel = div[c, x] * inverse
            if out is not None:
                out[c, x] = (2.0 * now[c, x] - old[c, x]) + (STEP_DT * STEP_DT) * accel
            if dotted is not None:
                term = dot_with[c, x] * accel
                summed = term if summed is None else summed + term
        if dotted is not None:
            dotted(x, summed)
        return carry

    lax.fori_loop(0, NX, plane, 0)


FIELD_SCRATCH = (
    pltpu.VMEM((3, NX + 16, NY + 16, NZ), F32),
    pltpu.VMEM((2, NX + 8, NY, NZ), F32),
    pltpu.VMEM((2, NX, 8, NZ), F32),
    pltpu.VMEM((3, NX + 8, NY, NZ), F32),
    pltpu.VMEM((3, NX, NY + 16, NZ), F32),
    pltpu.VMEM((3, NX, NY, NZ), F32),
    pltpu.VMEM((3, NX, NY, NZ), F32),
    pltpu.VMEM((2, 8, NY, NZ), F32),
    pltpu.VMEM((2, NX, 8, NZ), F32),
)


def first_s(
    start, station, wavelet, s, bulk_e, bulk_o, rows_e, rows_o, par_e, par_o,
    vp, vs, rho, old, a, s1, strain, k_rho, ext, lm, lmy, sx, sy, div, *depth,
):
    fill_field(ext, s, (bulk_e, bulk_o), (rows_e, rows_o), 0)
    fill_corner(ext, (par_e, par_o), 0)
    fill_lame(lm, lmy, vp, vs, rho, (par_e, par_o), (rows_e, rows_o))
    divergence(ext, lm, lmy, sx, sy, div, strain, *depth)
    add_source(div, station, wavelet, start, 1)

    def keep(x, value):
        k_rho[x] = value

    advance(s, old, div, rho, s1, a, keep)


def first_a(
    start, cells, counts, traces, a, bulk_e, bulk_o, rows_e, rows_o, par_e, par_o,
    vp, vs, rho, old, strain_s, a1, k_two, edge_e, edge_o,
    ext, lm, lmy, sx, sy, div, gz, gz_x, gz_y, strain,
):
    fill_field(ext, a, (bulk_e, bulk_o), (rows_e, rows_o), 3 * NX)
    fill_corner(ext, (par_e, par_o), 8)
    fill_lame(lm, lmy, vp, vs, rho, (par_e, par_o), (rows_e, rows_o))
    divergence(ext, lm, lmy, sx, sy, div, strain, gz, gz_x, gz_y)
    add_receivers(div, cells, counts, traces, start, 1)
    advance(a, old, div, rho, a1, None, None)
    right = even("gx")
    for c in range(3):
        for i in range(4):
            high, low = a1[c, NX - 4 + i], a1[c, i]
            edge_e[c, i] = jnp.where(right, high, low)
            edge_o[c, i] = jnp.where(right, low, high)

    def products(x, carry):
        e_a = [strain[slot, x] for slot in range(6)]
        e_s = [strain_s[slot, x] for slot in range(6)]
        lam, mu = correlate(e_a, e_s)
        k_two[0, x] = lam
        k_two[1, x] = mu
        return carry

    lax.fori_loop(0, NX, products, 0)


def correlate(e_a, e_s):
    trace_a = e_a[0] + e_a[3] + e_a[5]
    trace_s = e_s[0] + e_s[3] + e_s[5]
    mu = 0.5 * (e_a[0] * e_s[0] + e_a[3] * e_s[3] + e_a[5] * e_s[5])
    mu = mu + (e_a[1] * e_s[1] + e_a[2] * e_s[2] + e_a[4] * e_s[4])
    return 0.25 * (trace_a * trace_s), mu


def second_s(
    start, station, wavelet, s, bulk_e, bulk_o, rows_e, rows_o, first_e, first_o, par_e, par_o,
    vp, vs, rho, a, k_rho_first, strain, k_rho, ext, lm, lmy, sx, sy, div, *depth,
):
    fill_field(ext, s, (bulk_e, bulk_o), (rows_e, rows_o), 0)
    fill_rim(ext, (rows_e, rows_o))
    fill_lame(lm, lmy, vp, vs, rho, (par_e, par_o), (first_e, first_o))
    divergence(ext, lm, lmy, sx, sy, div, strain, *depth)
    add_source(div, station, wavelet, start, 0)

    def keep(x, value):
        k_rho[x] = k_rho_first[x] + value

    advance(s, None, div, rho, None, a, keep)


def second_a(parts, a, edge_e, edge_o, got_e, got_o, vp, vs, rho, strain_s, k_two, k_rho, *rest):
    outs, (ext, kernels) = rest[:parts], rest[parts:]
    matrix = band()
    ext[:, 4 : 4 + NX, 8 : 8 + NY, :] = a[...]

    def put_x(left, right):
        ext[:, 0:4, 8 : 8 + NY, :] = left[...]
        ext[:, 4 + NX : 8 + NX, 8 : 8 + NY, :] = right[...]

    ordered("gx", edge_e, edge_o, put_x)

    def put_rows(below, above):
        for c in range(3):
            for i in range(4):
                at = FOUR + c * 4 + i
                ext[c, 4 + i, 4:8, :] = below[at][:4]
                ext[c, 8 + i, 4:8, :] = below[at][4:]
                ext[c, 4 + i, 8 + NY : 12 + NY, :] = above[at][:4]
                ext[c, 8 + i, 8 + NY : 12 + NY, :] = above[at][4:]

    ordered("gy", got_e, got_o, put_rows)

    for c in range(3):
        kernels[c] = deriv_z(a[c], matrix)

    def plane(x, carry):
        e_a = all_strain(ext, x + 4, [kernels[j, x] for j in range(3)])
        lam, mu = correlate(e_a, [strain_s[slot, x] for slot in range(6)])
        lam = STEP_DT * (k_two[0, x] + lam)
        mu = STEP_DT * (k_two[1, x] + mu)
        density = rho[x]
        square_p, square_s = vp[x] * vp[x], vs[x] * vs[x]
        kernels[0, x] = 2.0 * density * square_p * lam
        kernels[1, x] = 2.0 * density * square_s * (mu - 2.0 * lam)
        kernels[2, x] = density * (
            STEP_DT * k_rho[x] + (square_p - 2.0 * square_s) * lam + square_s * mu
        )
        return carry

    lax.fori_loop(0, NX, plane, 0)
    share = NZ // parts
    lane = lax.broadcasted_iota(jnp.int32, (NY, NZ), 1)
    me = lax.axis_index("ens")
    for k in range(parts):
        first = share * jnp.bitwise_xor(me, k)

        def group(i, carry):
            kind, g = lax.div(i, NX // parts), lax.rem(i, NX // parts)
            packed = None
            for j in range(parts):
                shift = lax.rem(share * j - first + NZ, NZ)
                moved = pltpu.roll(kernels[kind, g * parts + j], shift, 1)
                packed = moved if packed is None else jnp.where(lane < share * j, packed, moved)
            outs[k][kind, g] = packed
            return carry

        lax.fori_loop(0, 3 * (NX // parts), group, 0)


def finish(parts, *refs):
    got, outs = refs[:parts], refs[parts:]
    share = NZ // parts
    for kind in range(3):
        for g in range(NX // parts):
            summed = got[0][kind, g]
            for k in range(1, parts):
                summed = summed + got[k][kind, g]
            for j in range(parts):
                moved = summed if j == 0 else pltpu.roll(summed, NZ - share * j, 1)
                outs[kind][g * parts + j] = moved[:, :share]


def swap(value, axis, odd):
    count = lax.axis_size(axis)
    pairs = [(i, i + 1) for i in range(odd, count - 1, 2)]
    return lax.ppermute(value, axis, pairs + [(j, i) for i, j in pairs])


def on_device(
    forward_now, forward_next, adjoint_now, adjoint_prev, speed_p, speed_s, density,
    station_cells, wavelets, receiver_cells, receiver_counts, adjoint_traces, start_step,
):
    s, old_s = forward_now[0], forward_next[0]
    a, old_a = adjoint_now[0], adjoint_prev[0]
    model = (speed_p, speed_s, density)
    start = start_step.reshape(1)
    work = 100_000_000
    tile = shapes(3, NX, NY, NZ)
    rows = call(
        pack_y, (shapes(7 * NX, 8, NZ),) * 2, s, a, *model,
        scratch=(pltpu.VMEM((2, 3, NX, 8, NZ), F32), pltpu.SemaphoreType.DMA((18,))),
        hbm=range(5), vmem=60,
    )
    rows = swap(rows[0], "gy", 0), swap(rows[1], "gy", 1)
    s_e, s_o = swap(s, "gx", 0), swap(s, "gx", 1)
    traces = adjoint_traces[0].transpose(1, 0, 2)
    sources = (station_cells, wavelets, receiver_cells, receiver_counts)
    par = call(
        pack_x, (shapes(48, 8, NZ),) * 2, *rows, *model, *sources, traces, smem=(5, 6, 7, 8)
    )
    a_sent = lax.optimization_barrier((a, par))[0]
    par = swap(par[0], "gx", 0), swap(par[1], "gx", 1)
    a_e, a_o = swap(a_sent, "gx", 0), swap(a_sent, "gx", 1)
    s1, strain_s, k_rho = call(
        first_s, (tile, shapes(6, NX, NY, NZ), shapes(NX, NY, NZ)),
        start, station_cells, wavelets, s, s_e, s_o, *rows, *par, *model, old_s, a,
        scratch=FIELD_SCRATCH, smem=(0, 1, 2), flops=work,
    )
    s1, a_e, a_o = lax.optimization_barrier((s1, a_e, a_o))
    s1_e, s1_o = swap(s1, "gx", 0), swap(s1, "gx", 1)
    edge = shapes(3, 4, NY, NZ)
    a1, k_two, edge_e, edge_o = call(
        first_a, (tile, shapes(2, NX, NY, NZ), edge, edge),
        start, receiver_cells, receiver_counts, traces,
        a, a_e, a_o, *rows, *par, *model, old_a, strain_s,
        scratch=FIELD_SCRATCH + (pltpu.VMEM((6, NX, NY, NZ), F32),), smem=(0, 1, 2), flops=work,
    )
    a1_e, a1_o = swap(edge_e, "gx", 0), swap(edge_o, "gx", 1)
    rim = call(pack_second, (shapes(FOUR + 12, 8, NZ),) * 2, s1, a1, s1_e, s1_o)
    rim = swap(rim[0], "gy", 0), swap(rim[1], "gy", 1)
    strain_s1, k_rho = call(
        second_s, (shapes(6, NX, NY, NZ), shapes(NX, NY, NZ)),
        start, station_cells, wavelets, s1, s1_e, s1_o, *rim, *rows, *par, *model, a1, k_rho,
        scratch=FIELD_SCRATCH, smem=(0, 1, 2), flops=work,
    )
    parts = lax.axis_size("ens")
    pieces = call(
        functools.partial(second_a, parts), (shapes(3, NX // parts, NY, NZ),) * parts,
        a1, a1_e, a1_o, *rim, *model, strain_s1, k_two, k_rho,
        scratch=(pltpu.VMEM((3, NX + 8, NY + 16, NZ), F32), pltpu.VMEM((3, NX, NY, NZ), F32)),
        flops=work,
    )
    got = [pieces[0]]
    for k in range(1, parts):
        got.append(lax.ppermute(pieces[k], "ens", [(i, i ^ k) for i in range(parts)]))
    return tuple(
        call(functools.partial(finish, parts), (shapes(NX, NY, NZ // parts),) * 3, *got)
    )


def solution(mesh):
    return jax.shard_map(
        on_device,
        mesh=mesh,
        in_specs=(
            P("ens", None, "gx", "gy", None),
            P("ens", None, "gx", "gy", None),
            P("ens", None, "gx", "gy", None),
            P("ens", None, "gx", "gy", None),
            P("gx", "gy", None),
            P("gx", "gy", None),
            P("gx", "gy", None),
            P("ens"),
            P("ens", None),
            P("ens", None),
            P("ens"),
            P("ens", None, None, None),
            P(),
        ),
        out_specs=(P("gx", "gy", "ens"), P("gx", "gy", "ens"), P("gx", "gy", "ens")),
        check_vma=False,
    )
```

```python
import functools

import jax
import jax.numpy as jnp
from jax import lax
from jax.experimental import pallas as pl
from jax.experimental.pallas import tpu as pltpu
from jax.sharding import PartitionSpec as P

COEF = (0.8, -0.2, 4.0 / 105.0, -1.0 / 280.0)
STEP_DT = 0.25
F32 = jnp.float32
PAIRS = ((0, 0), (0, 1), (0, 2), (1, 1), (1, 2), (2, 2))
SLOT = {(0, 0): 0, (0, 1): 1, (0, 2): 2, (1, 0): 1, (1, 1): 3, (1, 2): 4, (2, 0): 2, (2, 1): 4, (2, 2): 5}
NX, NY, NZ = 8, 32, 128


def shapes(*dims):
    return jax.ShapeDtypeStruct(dims, F32)


def call(body, out_shape, *args, scratch=(), smem=(), hbm=(), vmem=40, flops=10_000_000):
    specs = [pl.BlockSpec(memory_space=pltpu.VMEM) for _ in args]
    for i in smem:
        specs[i] = pl.BlockSpec(memory_space=pltpu.SMEM)
    for i in hbm:
        specs[i] = pl.BlockSpec(memory_space=pltpu.HBM)
    return pl.pallas_call(
        body,
        out_shape=out_shape,
        in_specs=specs,
        out_specs=jax.tree.map(lambda _: pl.BlockSpec(memory_space=pltpu.VMEM), out_shape),
        scratch_shapes=list(scratch),
        compiler_params=pltpu.CompilerParams(vmem_limit_bytes=vmem << 20),
        cost_estimate=pl.CostEstimate(flops=flops, bytes_accessed=1 << 20, transcendentals=0),
    )(*args)


def even(axis):
    return lax.rem(lax.axis_index(axis), 2) == 0


def band():
    step = lax.broadcasted_iota(jnp.int32, (NZ, NZ), 0) - lax.broadcasted_iota(jnp.int32, (NZ, NZ), 1)
    matrix = jnp.zeros((NZ, NZ), F32)
    for k, value in zip(range(1, 5), (672.0, -168.0, 32.0, -3.0)):
        matrix = matrix + jnp.where(step == k, value, 0.0) - jnp.where(step == -k, value, 0.0)
    return jnp.concatenate([matrix.astype(jnp.bfloat16)] * 3, axis=0)


def deriv_z(value, matrix):
    flat = value.reshape(-1, NZ)
    high = flat.astype(jnp.bfloat16)
    rest = flat - high.astype(F32)
    middle = rest.astype(jnp.bfloat16)
    low = (rest - middle.astype(F32)).astype(jnp.bfloat16)
    terms = jnp.concatenate([high, middle, low], axis=1)
    return (jnp.dot(terms, matrix, preferred_element_type=F32) * (1.0 / 840.0)).reshape(value.shape)


def deriv_x(ref, c, x, y0, rows):
    summed = None
    for k in range(1, 5):
        term = COEF[k - 1] * (ref[c, x + k, pl.ds(y0, rows), :] - ref[c, x - k, pl.ds(y0, rows), :])
        summed = term if summed is None else summed + term
    return summed


def deriv_y(ref, c, x, y0, rows):
    summed = None
    for k in range(1, 5):
        term = COEF[k - 1] * (ref[c, x, pl.ds(y0 + k, rows), :] - ref[c, x, pl.ds(y0 - k, rows), :])
        summed = term if summed is None else summed + term
    return summed


def lame(vp, vs, rho):
    square_s = vs * vs
    return rho * (vp * vp - 2.0 * square_s), rho * square_s


def ordered(axis, got_even, got_odd, put):
    @pl.when(even(axis))
    def _():
        put(got_odd, got_even)

    @pl.when(jnp.logical_not(even(axis)))
    def _():
        put(got_even, got_odd)


def edge_rows(tile, out_e, out_o, base):
    upper = even("gy")
    for c in range(3):
        for x in range(NX):
            high, low = tile[c, x, NY - 8 :, :], tile[c, x, :8, :]
            out_e[base + c * NX + x] = jnp.where(upper, high, low)
            out_o[base + c * NX + x] = jnp.where(upper, low, high)


def pack_y(s, a, vp, vs, rho, out_e, out_o, model, sems):
    upper = even("gy")
    start = jnp.where(upper, NY - 8, 0)
    copies = []

    def begin(src, dst):
        copies.append(pltpu.make_async_copy(src, dst, sems.at[len(copies)]))
        copies[-1].start()

    for out, first in ((out_e, start), (out_o, NY - 8 - start)):
        rows = pl.ds(pl.multiple_of(first, 8), 8)
        for f, field in enumerate((s, a)):
            for c in range(3):
                at = (f * 3 + c) * NX
                begin(field.at[c, :, rows, :], out.at[at : at + NX])
        for i, field in enumerate((vp, vs, rho)):
            begin(field.at[:, rows, :], model.at[0 if out is out_e else 1, i])
    for copy in copies:
        copy.wait()
    for x in range(NX):
        for side, out in ((0, out_e), (1, out_o)):
            lam, mu = lame(model[side, 0, x], model[side, 1, x], model[side, 2, x])
            high = jnp.concatenate([lam[4:], mu[4:]], axis=0)
            low = jnp.concatenate([lam[:4], mu[:4]], axis=0)
            out[6 * NX + x] = jnp.where(upper if side == 0 else jnp.logical_not(upper), high, low)


def pack_corner_rows(got_e, got_o, out_e, out_o, fields):
    def put(below, above):
        right = even("gx")
        for f in range(fields):
            for c in range(2):
                for i in range(4):
                    row = [None, None]
                    for side, x in ((0, i), (1, NX - 4 + i)):
                        at = (f * 3 + c) * NX + x
                        row[side] = jnp.concatenate([below[at][4:], above[at][:4]], axis=0)
                    slot = (f * 2 + c) * 4 + i
                    out_e[slot] = jnp.where(right, row[1], row[0])
                    out_o[slot] = jnp.where(right, row[0], row[1])

    ordered("gy", got_e, got_o, put)


def pack_x(got_e, got_o, vp, vs, rho, station, wavelet, cells, counts, traces, out_e, out_o):
    pack_corner_rows(got_e, got_o, out_e, out_o, 2)
    right = even("gx")
    for i in range(4):
        low = lame(vp[i], vs[i], rho[i])
        high = lame(vp[NX - 4 + i], vs[NX - 4 + i], rho[NX - 4 + i])
        for which in range(2):
            for part in range(4):
                rows = slice(8 * part, 8 * part + 8)
                slot = 16 + (which * 4 + i) * 4 + part
                out_e[slot] = jnp.where(right, high[which][rows], low[which][rows])
                out_o[slot] = jnp.where(right, low[which][rows], high[which][rows])


RIM = 3 * NX
FOUR = RIM + 8


def pack_second(s1, a1, bulk_e, bulk_o, out_e, out_o):
    edge_rows(s1, out_e, out_o, 0)
    upper = even("gy")

    def put(left, right):
        for c in range(2):
            for i in range(4):
                before, after = left[c, NX - 4 + i], right[c, i]
                high = jnp.concatenate([before[NY - 4 :], after[NY - 4 :]], axis=0)
                low = jnp.concatenate([before[:4], after[:4]], axis=0)
                out_e[RIM + c * 4 + i] = jnp.where(upper, high, low)
                out_o[RIM + c * 4 + i] = jnp.where(upper, low, high)

    ordered("gx", bulk_e, bulk_o, put)
    for c in range(3):
        for i in range(4):
            high = jnp.concatenate([a1[c, i, NY - 4 :, :], a1[c, i + 4, NY - 4 :, :]], axis=0)
            low = jnp.concatenate([a1[c, i, :4, :], a1[c, i + 4, :4, :]], axis=0)
            out_e[FOUR + c * 4 + i] = jnp.where(upper, high, low)
            out_o[FOUR + c * 4 + i] = jnp.where(upper, low, high)


def fill_field(ext, tile, bulk, rows, base):
    ext[:, 8 : 8 + NX, 8 : 8 + NY, :] = tile[...]

    def put_x(left, right):
        ext[:, 0:8, 8 : 8 + NY, :] = left[...]
        ext[:, 8 + NX : 16 + NX, 8 : 8 + NY, :] = right[...]

    ordered("gx", bulk[0], bulk[1], put_x)

    def put_rows(below, above):
        for c in range(3):
            for x in range(NX):
                ext[c, 8 + x, 0:8, :] = below[base + c * NX + x]
                ext[c, 8 + x, 8 + NY : 16 + NY, :] = above[base + c * NX + x]

    ordered("gy", rows[0], rows[1], put_rows)


def fill_corner(ext, got, base):
    def put(left, right):
        for c in range(2):
            for i in range(4):
                at = base + c * 4 + i
                ext[c, 4 + i, 4:8, :] = left[at][:4]
                ext[c, 4 + i, 8 + NY : 12 + NY, :] = left[at][4:]
                ext[c, 8 + NX + i, 4:8, :] = right[at][:4]
                ext[c, 8 + NX + i, 8 + NY : 12 + NY, :] = right[at][4:]

    ordered("gx", got[0], got[1], put)


def fill_rim(ext, rows):
    def put(below, above):
        for c in range(2):
            for i in range(4):
                at = RIM + c * 4 + i
                ext[c, 4 + i, 4:8, :] = below[at][:4]
                ext[c, 8 + NX + i, 4:8, :] = below[at][4:]
                ext[c, 4 + i, 8 + NY : 12 + NY, :] = above[at][:4]
                ext[c, 8 + NX + i, 8 + NY : 12 + NY, :] = above[at][4:]

    ordered("gy", rows[0], rows[1], put)


def fill_lame(lm, lmy, vp, vs, rho, planes, rows):
    for x in range(NX):
        lam, mu = lame(vp[x], vs[x], rho[x])
        lm[0, 4 + x] = lam
        lm[1, 4 + x] = mu

    def put_x(left, right):
        for which in range(2):
            for i in range(4):
                for part in range(4):
                    at = 16 + (which * 4 + i) * 4 + part
                    lm[which, i, 8 * part : 8 * part + 8, :] = left[at]
                    lm[which, 4 + NX + i, 8 * part : 8 * part + 8, :] = right[at]

    ordered("gx", planes[0], planes[1], put_x)

    def put_rows(below, above):
        lmy[0] = below[6 * NX : 7 * NX]
        lmy[1] = above[6 * NX : 7 * NX]

    ordered("gy", rows[0], rows[1], put_rows)


def all_strain(ext, x, gz):
    g = [[None] * 3 for _ in range(3)]
    for j in range(3):
        g[0][j] = deriv_x(ext, j, x, 8, NY)
        g[1][j] = deriv_y(ext, j, x, 8, NY)
        g[2][j] = gz[j]
    return [g[i][j] + g[j][i] for i, j in PAIRS]


def divergence(ext, lm, lmy, sx, sy, div, strain, gz, gz_x, gz_y):
    matrix = band()
    for c in range(3):
        gz[c] = deriv_z(ext[c, 8 : 8 + NX, 8 : 8 + NY, :], matrix)
    for slot, c in enumerate((0, 2)):
        planes = [ext[c, 4:8, 8 : 8 + NY, :], ext[c, 8 + NX : 12 + NX, 8 : 8 + NY, :]]
        gz_x[slot] = deriv_z(jnp.concatenate(planes, axis=0), matrix)
    for slot, c in enumerate((1, 2)):
        rows = [ext[c, 8 : 8 + NX, 4:8, :], ext[c, 8 : 8 + NX, 8 + NY : 12 + NY, :]]
        gz_y[slot] = deriv_z(jnp.concatenate(rows, axis=1), matrix)

    def halo_plane(i, carry):
        x = jnp.where(i < 4, i, i + NX)
        xe = x + 4
        lam, mu = lm[0, x], lm[1, x]
        g00 = deriv_x(ext, 0, xe, 8, NY)
        g11 = deriv_y(ext, 1, xe, 8, NY)
        sx[0, x] = lam * (g00 + g11 + gz_x[1, i]) + mu * (g00 + g00)
        sx[1, x] = mu * (deriv_x(ext, 1, xe, 8, NY) + deriv_y(ext, 0, xe, 8, NY))
        sx[2, x] = mu * (deriv_x(ext, 2, xe, 8, NY) + gz_x[0, i])
        return carry

    lax.fori_loop(0, 8, halo_plane, 0)

    def plane(x, carry):
        xe = x + 8
        lam, mu = lm[0, x + 4], lm[1, x + 4]
        e = all_strain(ext, xe, [gz[j, x] for j in range(3)])
        for slot in range(6):
            strain[slot, x] = e[slot]
        pressure = lam * (0.5 * (e[0] + e[3] + e[5]))
        sx[0, x + 4] = pressure + mu * e[0]
        shear = mu * e[1]
        sx[1, x + 4] = shear
        sy[0, x, 8 : 8 + NY, :] = shear
        shear = mu * e[2]
        sx[2, x + 4] = shear
        gz[0, x] = shear
        sy[1, x, 8 : 8 + NY, :] = pressure + mu * e[3]
        shear = mu * e[4]
        sy[2, x, 8 : 8 + NY, :] = shear
        gz[1, x] = shear
        gz[2, x] = pressure + mu * e[5]
        for side, y0 in ((0, 4), (1, 8 + NY)):
            both = lmy[side, x]
            lam4, mu4 = both[:4], both[4:]
            g00 = deriv_x(ext, 0, xe, y0, 4)
            g11 = deriv_y(ext, 1, xe, y0, 4)
            rows = slice(4 * side, 4 * side + 4)
            sy[0, x, y0 : y0 + 4, :] = mu4 * (
                deriv_x(ext, 1, xe, y0, 4) + deriv_y(ext, 0, xe, y0, 4)
            )
            sy[1, x, y0 : y0 + 4, :] = lam4 * (g00 + g11 + gz_y[1, x, rows, :]) + mu4 * (g11 + g11)
            sy[2, x, y0 : y0 + 4, :] = mu4 * (
                deriv_y(ext, 2, xe, y0, 4) + gz_y[0, x, rows, :]
            )
        return carry

    lax.fori_loop(0, NX, plane, 0)
    for c in range(3):
        div[c] = deriv_z(gz[c], matrix)

    def close(x, carry):
        for c in range(3):
            div[c, x] = div[c, x] + (
                deriv_x(sx, c, x + 4, 0, NY) + deriv_y(sy, c, x, 8, NY)
            )
        return carry

    lax.fori_loop(0, NX, close, 0)


def locate(cell):
    plane = lax.axis_size("gy") * NY * NZ
    ix = lax.div(cell, plane) - lax.axis_index("gx") * NX
    iy = lax.rem(lax.div(cell, NZ), lax.axis_size("gy") * NY) - lax.axis_index("gy") * NY
    iz = lax.rem(cell, NZ)
    inside = (ix >= 0) & (ix < NX) & (iy >= 0) & (iy < NY)
    return ix, iy, iz, inside


def add_force(div, c, ix, iy, iz, amount):
    lane = lax.broadcasted_iota(jnp.int32, (1, NZ), 1)
    row = div[c, ix, pl.ds(iy, 1), :]
    div[c, ix, pl.ds(iy, 1), :] = row + jnp.where(lane == iz, amount, 0.0)


def add_source(div, station, wavelet, start, offset):
    ix, iy, iz, inside = locate(station[0])

    @pl.when(inside)
    def _():
        add_force(div, 2, ix, iy, iz, wavelet[0, start[0] + offset])


def add_receivers(div, cells, counts, traces, start, offset):
    moment = start[0] + offset
    time = lax.broadcasted_iota(jnp.int32, (3, traces.shape[2]), 1)

    def one(r, carry):
        ix, iy, iz, inside = locate(cells[0, r])

        @pl.when(inside)
        def _():
            amounts = jnp.sum(
                jnp.where(time == moment, traces[:, r, :], 0.0), axis=1, keepdims=True
            )
            for c in range(3):
                add_force(div, c, ix, iy, iz, amounts[c : c + 1])

        return carry

    lax.fori_loop(0, counts[0], one, 0)


def advance(now, old, div, rho, out, dot_with, dotted):
    def plane(x, carry):
        inverse = 1.0 / rho[x]
        summed = None
        for c in range(3):
            accel = div[c, x] * inverse
            if out is not None:
                out[c, x] = (2.0 * now[c, x] - old[c, x]) + (STEP_DT * STEP_DT) * accel
            if dotted is not None:
                term = dot_with[c, x] * accel
                summed = term if summed is None else summed + term
        if dotted is not None:
            dotted(x, summed)
        return carry

    lax.fori_loop(0, NX, plane, 0)


FIELD_SCRATCH = (
    pltpu.VMEM((3, NX + 16, NY + 16, NZ), F32),
    pltpu.VMEM((2, NX + 8, NY, NZ), F32),
    pltpu.VMEM((2, NX, 8, NZ), F32),
    pltpu.VMEM((3, NX + 8, NY, NZ), F32),
    pltpu.VMEM((3, NX, NY + 16, NZ), F32),
    pltpu.VMEM((3, NX, NY, NZ), F32),
    pltpu.VMEM((3, NX, NY, NZ), F32),
    pltpu.VMEM((2, 8, NY, NZ), F32),
    pltpu.VMEM((2, NX, 8, NZ), F32),
)


def first_s(
    start, station, wavelet, s, bulk_e, bulk_o, rows_e, rows_o, par_e, par_o,
    vp, vs, rho, old, a, s1, strain, k_rho, ext, lm, lmy, sx, sy, div, *depth,
):
    fill_field(ext, s, (bulk_e, bulk_o), (rows_e, rows_o), 0)
    fill_corner(ext, (par_e, par_o), 0)
    fill_lame(lm, lmy, vp, vs, rho, (par_e, par_o), (rows_e, rows_o))
    divergence(ext, lm, lmy, sx, sy, div, strain, *depth)
    add_source(div, station, wavelet, start, 1)

    def keep(x, value):
        k_rho[x] = value

    advance(s, old, div, rho, s1, a, keep)


def first_a(
    start, cells, counts, traces, a, bulk_e, bulk_o, rows_e, rows_o, par_e, par_o,
    vp, vs, rho, old, strain_s, a1, k_two, edge_e, edge_o,
    ext, lm, lmy, sx, sy, div, gz, gz_x, gz_y, strain,
):
    fill_field(ext, a, (bulk_e, bulk_o), (rows_e, rows_o), 3 * NX)
    fill_corner(ext, (par_e, par_o), 8)
    fill_lame(lm, lmy, vp, vs, rho, (par_e, par_o), (rows_e, rows_o))
    divergence(ext, lm, lmy, sx, sy, div, strain, gz, gz_x, gz_y)
    add_receivers(div, cells, counts, traces, start, 1)
    advance(a, old, div, rho, a1, None, None)
    right = even("gx")
    for c in range(3):
        for i in range(4):
            high, low = a1[c, NX - 4 + i], a1[c, i]
            edge_e[c, i] = jnp.where(right, high, low)
            edge_o[c, i] = jnp.where(right, low, high)

    def products(x, carry):
        e_a = [strain[slot, x] for slot in range(6)]
        e_s = [strain_s[slot, x] for slot in range(6)]
        lam, mu = correlate(e_a, e_s)
        k_two[0, x] = lam
        k_two[1, x] = mu
        return carry

    lax.fori_loop(0, NX, products, 0)


def correlate(e_a, e_s):
    trace_a = e_a[0] + e_a[3] + e_a[5]
    trace_s = e_s[0] + e_s[3] + e_s[5]
    mu = 0.5 * (e_a[0] * e_s[0] + e_a[3] * e_s[3] + e_a[5] * e_s[5])
    mu = mu + (e_a[1] * e_s[1] + e_a[2] * e_s[2] + e_a[4] * e_s[4])
    return 0.25 * (trace_a * trace_s), mu


def fill_adjoint(ext, a1, edges, rows):
    ext[:, 8 : 8 + NX, 8 : 8 + NY, :] = a1[...]

    def put_x(left, right):
        ext[:, 4:8, 8 : 8 + NY, :] = left[...]
        ext[:, 8 + NX : 12 + NX, 8 : 8 + NY, :] = right[...]

    ordered("gx", edges[0], edges[1], put_x)

    def put_rows(below, above):
        for c in range(3):
            for i in range(4):
                at = FOUR + c * 4 + i
                ext[c, 8 + i, 4:8, :] = below[at][:4]
                ext[c, 12 + i, 4:8, :] = below[at][4:]
                ext[c, 8 + i, 8 + NY : 12 + NY, :] = above[at][:4]
                ext[c, 12 + i, 8 + NY : 12 + NY, :] = above[at][4:]

    ordered("gy", rows[0], rows[1], put_rows)


def second_step(
    parts, start, station, wavelet, s, s_e, s_o, a, a_e, a_o, rows_e, rows_o, first_e, first_o,
    par_e, par_o, vp, vs, rho, k_two, k_first, *rest,
):
    outs, (ext, lm, lmy, sx, sy, div, gz, gz_x, gz_y, strain, k_rho, kernels) = (
        rest[:parts], rest[parts:]
    )
    fill_lame(lm, lmy, vp, vs, rho, (par_e, par_o), (first_e, first_o))
    fill_field(ext, s, (s_e, s_o), (rows_e, rows_o), 0)
    fill_rim(ext, (rows_e, rows_o))
    divergence(ext, lm, lmy, sx, sy, div, strain, gz, gz_x, gz_y)
    add_source(div, station, wavelet, start, 0)

    def keep(x, value):
        k_rho[x] = k_first[x] + value

    advance(s, None, div, rho, None, a, keep)
    fill_adjoint(ext, a, (a_e, a_o), (rows_e, rows_o))
    matrix = band()
    for c in range(3):
        gz[c] = deriv_z(a[c], matrix)

    def plane(x, carry):
        e_a = all_strain(ext, x + 8, [gz[j, x] for j in range(3)])
        lam, mu = correlate(e_a, [strain[slot, x] for slot in range(6)])
        lam = STEP_DT * (k_two[0, x] + lam)
        mu = STEP_DT * (k_two[1, x] + mu)
        density = rho[x]
        square_p, square_s = vp[x] * vp[x], vs[x] * vs[x]
        kernels[0, x] = 2.0 * density * square_p * lam
        kernels[1, x] = 2.0 * density * square_s * (mu - 2.0 * lam)
        kernels[2, x] = density * (
            STEP_DT * k_rho[x] + (square_p - 2.0 * square_s) * lam + square_s * mu
        )
        return carry

    lax.fori_loop(0, NX, plane, 0)
    share = NZ // parts
    lane = lax.broadcasted_iota(jnp.int32, (NY, NZ), 1)
    me = lax.axis_index("ens")
    for k in range(parts):
        first = share * jnp.bitwise_xor(me, k)

        def group(i, carry):
            kind, g = lax.div(i, NX // parts), lax.rem(i, NX // parts)
            packed = None
            for j in range(parts):
                shift = lax.rem(share * j - first + NZ, NZ)
                moved = pltpu.roll(kernels[kind, g * parts + j], shift, 1)
                packed = moved if packed is None else jnp.where(lane < share * j, packed, moved)
            outs[k][kind, g] = packed
            return carry

        lax.fori_loop(0, 3 * (NX // parts), group, 0)


def finish(parts, *refs):
    got, outs = refs[:parts], refs[parts:]
    share = NZ // parts
    for kind in range(3):
        for g in range(NX // parts):
            summed = got[0][kind, g]
            for k in range(1, parts):
                summed = summed + got[k][kind, g]
            for j in range(parts):
                moved = summed if j == 0 else pltpu.roll(summed, NZ - share * j, 1)
                outs[kind][g * parts + j] = moved[:, :share]


def swap(value, axis, odd):
    count = lax.axis_size(axis)
    pairs = [(i, i + 1) for i in range(odd, count - 1, 2)]
    return lax.ppermute(value, axis, pairs + [(j, i) for i, j in pairs])


def on_device(
    forward_now, forward_next, adjoint_now, adjoint_prev, speed_p, speed_s, density,
    station_cells, wavelets, receiver_cells, receiver_counts, adjoint_traces, start_step,
):
    s, old_s = forward_now[0], forward_next[0]
    a, old_a = adjoint_now[0], adjoint_prev[0]
    model = (speed_p, speed_s, density)
    start = start_step.reshape(1)
    work = 100_000_000
    tile = shapes(3, NX, NY, NZ)
    rows = call(
        pack_y, (shapes(7 * NX, 8, NZ),) * 2, s, a, *model,
        scratch=(pltpu.VMEM((2, 3, NX, 8, NZ), F32), pltpu.SemaphoreType.DMA((18,))),
        hbm=range(5), vmem=60,
    )
    rows = swap(rows[0], "gy", 0), swap(rows[1], "gy", 1)
    s_e, s_o = swap(s, "gx", 0), swap(s, "gx", 1)
    traces = adjoint_traces[0].transpose(1, 0, 2)
    sources = (station_cells, wavelets, receiver_cells, receiver_counts)
    par = call(
        pack_x, (shapes(48, 8, NZ),) * 2, *rows, *model, *sources, traces, smem=(5, 6, 7, 8)
    )
    a_sent = lax.optimization_barrier((a, par))[0]
    par = swap(par[0], "gx", 0), swap(par[1], "gx", 1)
    a_e, a_o = swap(a_sent, "gx", 0), swap(a_sent, "gx", 1)
    s1, strain_s, k_rho = call(
        first_s, (tile, shapes(6, NX, NY, NZ), shapes(NX, NY, NZ)),
        start, station_cells, wavelets, s, s_e, s_o, *rows, *par, *model, old_s, a,
        scratch=FIELD_SCRATCH, smem=(0, 1, 2), flops=work,
    )
    s1, a_e, a_o = lax.optimization_barrier((s1, a_e, a_o))
    s1_e, s1_o = swap(s1, "gx", 0), swap(s1, "gx", 1)
    edge = shapes(3, 4, NY, NZ)
    a1, k_two, edge_e, edge_o = call(
        first_a, (tile, shapes(2, NX, NY, NZ), edge, edge),
        start, receiver_cells, receiver_counts, traces,
        a, a_e, a_o, *rows, *par, *model, old_a, strain_s,
        scratch=FIELD_SCRATCH + (pltpu.VMEM((6, NX, NY, NZ), F32),), smem=(0, 1, 2), flops=work,
    )
    a1_e, a1_o = swap(edge_e, "gx", 0), swap(edge_o, "gx", 1)
    rim = call(pack_second, (shapes(FOUR + 12, 8, NZ),) * 2, s1, a1, s1_e, s1_o)
    rim = swap(rim[0], "gy", 0), swap(rim[1], "gy", 1)
    parts = lax.axis_size("ens")
    pieces = call(
        functools.partial(second_step, parts), (shapes(3, NX // parts, NY, NZ),) * parts,
        start, station_cells, wavelets, s1, s1_e, s1_o, a1, a1_e, a1_o, *rim, *rows, *par, *model,
        k_two, k_rho,
        scratch=FIELD_SCRATCH + (
            pltpu.VMEM((6, NX, NY, NZ), F32), pltpu.VMEM((NX, NY, NZ), F32),
            pltpu.VMEM((3, NX, NY, NZ), F32),
        ),
        smem=(0, 1, 2), flops=work,
    )
    got = [pieces[0]]
    for k in range(1, parts):
        got.append(lax.ppermute(pieces[k], "ens", [(i, i ^ k) for i in range(parts)]))
    return tuple(
        call(functools.partial(finish, parts), (shapes(NX, NY, NZ // parts),) * 3, *got)
    )


def solution(mesh):
    return jax.shard_map(
        on_device,
        mesh=mesh,
        in_specs=(
            P("ens", None, "gx", "gy", None),
            P("ens", None, "gx", "gy", None),
            P("ens", None, "gx", "gy", None),
            P("ens", None, "gx", "gy", None),
            P("gx", "gy", None),
            P("gx", "gy", None),
            P("gx", "gy", None),
            P("ens"),
            P("ens", None),
            P("ens", None),
            P("ens"),
            P("ens", None, None, None),
            P(),
        ),
        out_specs=(P("gx", "gy", "ens"), P("gx", "gy", "ens"), P("gx", "gy", "ens")),
        check_vma=False,
    )
```

```python
import functools

import jax
import jax.numpy as jnp
from jax import lax
from jax.experimental import pallas as pl
from jax.experimental.pallas import tpu as pltpu
from jax.sharding import PartitionSpec as P

COEF = (0.8, -0.2, 4.0 / 105.0, -1.0 / 280.0)
STEP_DT = 0.25
F32 = jnp.float32
PAIRS = ((0, 0), (0, 1), (0, 2), (1, 1), (1, 2), (2, 2))
SLOT = {(0, 0): 0, (0, 1): 1, (0, 2): 2, (1, 0): 1, (1, 1): 3, (1, 2): 4, (2, 0): 2, (2, 1): 4, (2, 2): 5}
NX, NY, NZ = 8, 32, 128


def shapes(*dims):
    return jax.ShapeDtypeStruct(dims, F32)


def call(body, out_shape, *args, scratch=(), smem=(), hbm=(), vmem=40, flops=10_000_000):
    specs = [pl.BlockSpec(memory_space=pltpu.VMEM) for _ in args]
    for i in smem:
        specs[i] = pl.BlockSpec(memory_space=pltpu.SMEM)
    for i in hbm:
        specs[i] = pl.BlockSpec(memory_space=pltpu.HBM)
    return pl.pallas_call(
        body,
        out_shape=out_shape,
        in_specs=specs,
        out_specs=jax.tree.map(lambda _: pl.BlockSpec(memory_space=pltpu.VMEM), out_shape),
        scratch_shapes=list(scratch),
        compiler_params=pltpu.CompilerParams(vmem_limit_bytes=vmem << 20),
        cost_estimate=pl.CostEstimate(flops=flops, bytes_accessed=1 << 20, transcendentals=0),
    )(*args)


def even(axis):
    return lax.rem(lax.axis_index(axis), 2) == 0


def band():
    step = lax.broadcasted_iota(jnp.int32, (NZ, NZ), 0) - lax.broadcasted_iota(jnp.int32, (NZ, NZ), 1)
    matrix = jnp.zeros((NZ, NZ), F32)
    for k, value in zip(range(1, 5), (672.0, -168.0, 32.0, -3.0)):
        matrix = matrix + jnp.where(step == k, value, 0.0) - jnp.where(step == -k, value, 0.0)
    return jnp.concatenate([matrix.astype(jnp.bfloat16)] * 3, axis=0)


def deriv_z(value, matrix):
    flat = value.reshape(-1, NZ)
    high = flat.astype(jnp.bfloat16)
    rest = flat - high.astype(F32)
    middle = rest.astype(jnp.bfloat16)
    low = (rest - middle.astype(F32)).astype(jnp.bfloat16)
    terms = jnp.concatenate([high, middle, low], axis=1)
    return (jnp.dot(terms, matrix, preferred_element_type=F32) * (1.0 / 840.0)).reshape(value.shape)


def deriv_x(ref, c, x, y0, rows):
    summed = None
    for k in range(1, 5):
        term = COEF[k - 1] * (ref[c, x + k, pl.ds(y0, rows), :] - ref[c, x - k, pl.ds(y0, rows), :])
        summed = term if summed is None else summed + term
    return summed


def deriv_y(ref, c, x, y0, rows):
    summed = None
    for k in range(1, 5):
        term = COEF[k - 1] * (ref[c, x, pl.ds(y0 + k, rows), :] - ref[c, x, pl.ds(y0 - k, rows), :])
        summed = term if summed is None else summed + term
    return summed


def lame(vp, vs, rho):
    square_s = vs * vs
    return rho * (vp * vp - 2.0 * square_s), rho * square_s


def ordered(axis, got_even, got_odd, put):
    @pl.when(even(axis))
    def _():
        put(got_odd, got_even)

    @pl.when(jnp.logical_not(even(axis)))
    def _():
        put(got_even, got_odd)


def edge_rows(tile, out_e, out_o, base):
    upper = even("gy")
    for c in range(3):
        for x in range(NX):
            high, low = tile[c, x, NY - 8 :, :], tile[c, x, :8, :]
            out_e[base + c * NX + x] = jnp.where(upper, high, low)
            out_o[base + c * NX + x] = jnp.where(upper, low, high)


def pack_y(s, a, vp, vs, rho, out_e, out_o, model, sems):
    upper = even("gy")
    start = jnp.where(upper, NY - 8, 0)
    copies = []

    def begin(src, dst):
        copies.append(pltpu.make_async_copy(src, dst, sems.at[len(copies)]))
        copies[-1].start()

    for out, first in ((out_e, start), (out_o, NY - 8 - start)):
        rows = pl.ds(pl.multiple_of(first, 8), 8)
        for f, field in enumerate((s, a)):
            for c in range(3):
                at = (f * 3 + c) * NX
                begin(field.at[c, :, rows, :], out.at[at : at + NX])
        for i, field in enumerate((vp, vs, rho)):
            begin(field.at[:, rows, :], model.at[0 if out is out_e else 1, i])
    for copy in copies:
        copy.wait()
    for x in range(NX):
        for side, out in ((0, out_e), (1, out_o)):
            lam, mu = lame(model[side, 0, x], model[side, 1, x], model[side, 2, x])
            high = jnp.concatenate([lam[4:], mu[4:]], axis=0)
            low = jnp.concatenate([lam[:4], mu[:4]], axis=0)
            out[6 * NX + x] = jnp.where(upper if side == 0 else jnp.logical_not(upper), high, low)


def pack_corner_rows(got_e, got_o, out_e, out_o, fields):
    def put(below, above):
        right = even("gx")
        for f in range(fields):
            for c in range(2):
                for i in range(4):
                    row = [None, None]
                    for side, x in ((0, i), (1, NX - 4 + i)):
                        at = (f * 3 + c) * NX + x
                        row[side] = jnp.concatenate([below[at][4:], above[at][:4]], axis=0)
                    slot = (f * 2 + c) * 4 + i
                    out_e[slot] = jnp.where(right, row[1], row[0])
                    out_o[slot] = jnp.where(right, row[0], row[1])

    ordered("gy", got_e, got_o, put)


def pack_x(got_e, got_o, vp, vs, rho, station, wavelet, cells, counts, traces, out_e, out_o):
    pack_corner_rows(got_e, got_o, out_e, out_o, 2)
    right = even("gx")
    for i in range(4):
        low = lame(vp[i], vs[i], rho[i])
        high = lame(vp[NX - 4 + i], vs[NX - 4 + i], rho[NX - 4 + i])
        for which in range(2):
            for part in range(4):
                rows = slice(8 * part, 8 * part + 8)
                slot = 16 + (which * 4 + i) * 4 + part
                out_e[slot] = jnp.where(right, high[which][rows], low[which][rows])
                out_o[slot] = jnp.where(right, low[which][rows], high[which][rows])


RIM = 3 * NX
FOUR = RIM + 8


def pack_second(s1, a1, bulk_e, bulk_o, out_e, out_o):
    edge_rows(s1, out_e, out_o, 0)
    upper = even("gy")

    def put(left, right):
        for c in range(2):
            for i in range(4):
                before, after = left[c, NX - 4 + i], right[c, i]
                high = jnp.concatenate([before[NY - 4 :], after[NY - 4 :]], axis=0)
                low = jnp.concatenate([before[:4], after[:4]], axis=0)
                out_e[RIM + c * 4 + i] = jnp.where(upper, high, low)
                out_o[RIM + c * 4 + i] = jnp.where(upper, low, high)

    ordered("gx", bulk_e, bulk_o, put)
    for c in range(3):
        for i in range(4):
            high = jnp.concatenate([a1[c, i, NY - 4 :, :], a1[c, i + 4, NY - 4 :, :]], axis=0)
            low = jnp.concatenate([a1[c, i, :4, :], a1[c, i + 4, :4, :]], axis=0)
            out_e[FOUR + c * 4 + i] = jnp.where(upper, high, low)
            out_o[FOUR + c * 4 + i] = jnp.where(upper, low, high)


def fill_field(ext, tile, bulk, rows, base):
    ext[:, 8 : 8 + NX, 8 : 8 + NY, :] = tile[...]

    def put_x(left, right):
        ext[:, 0:8, 8 : 8 + NY, :] = left[...]
        ext[:, 8 + NX : 16 + NX, 8 : 8 + NY, :] = right[...]

    ordered("gx", bulk[0], bulk[1], put_x)

    def put_rows(below, above):
        for c in range(3):
            for x in range(NX):
                ext[c, 8 + x, 0:8, :] = below[base + c * NX + x]
                ext[c, 8 + x, 8 + NY : 16 + NY, :] = above[base + c * NX + x]

    ordered("gy", rows[0], rows[1], put_rows)


def fill_corner(ext, got, base):
    def put(left, right):
        for c in range(2):
            for i in range(4):
                at = base + c * 4 + i
                ext[c, 4 + i, 4:8, :] = left[at][:4]
                ext[c, 4 + i, 8 + NY : 12 + NY, :] = left[at][4:]
                ext[c, 8 + NX + i, 4:8, :] = right[at][:4]
                ext[c, 8 + NX + i, 8 + NY : 12 + NY, :] = right[at][4:]

    ordered("gx", got[0], got[1], put)


def fill_rim(ext, rows):
    def put(below, above):
        for c in range(2):
            for i in range(4):
                at = RIM + c * 4 + i
                ext[c, 4 + i, 4:8, :] = below[at][:4]
                ext[c, 8 + NX + i, 4:8, :] = below[at][4:]
                ext[c, 4 + i, 8 + NY : 12 + NY, :] = above[at][:4]
                ext[c, 8 + NX + i, 8 + NY : 12 + NY, :] = above[at][4:]

    ordered("gy", rows[0], rows[1], put)


def fill_lame(lm, lmy, vp, vs, rho, planes, rows):
    for x in range(NX):
        lam, mu = lame(vp[x], vs[x], rho[x])
        lm[0, 4 + x] = lam
        lm[1, 4 + x] = mu

    def put_x(left, right):
        for which in range(2):
            for i in range(4):
                for part in range(4):
                    at = 16 + (which * 4 + i) * 4 + part
                    lm[which, i, 8 * part : 8 * part + 8, :] = left[at]
                    lm[which, 4 + NX + i, 8 * part : 8 * part + 8, :] = right[at]

    ordered("gx", planes[0], planes[1], put_x)

    def put_rows(below, above):
        lmy[0] = below[6 * NX : 7 * NX]
        lmy[1] = above[6 * NX : 7 * NX]

    ordered("gy", rows[0], rows[1], put_rows)


def all_strain(ext, x, gz):
    g = [[None] * 3 for _ in range(3)]
    for j in range(3):
        g[0][j] = deriv_x(ext, j, x, 8, NY)
        g[1][j] = deriv_y(ext, j, x, 8, NY)
        g[2][j] = gz[j]
    return [g[i][j] + g[j][i] for i, j in PAIRS]


def divergence(ext, lm, lmy, sx, sy, div, strain, gz, gz_x, gz_y):
    matrix = band()
    for c in range(3):
        gz[c] = deriv_z(ext[c, 8 : 8 + NX, 8 : 8 + NY, :], matrix)
    for slot, c in enumerate((0, 2)):
        planes = [ext[c, 4:8, 8 : 8 + NY, :], ext[c, 8 + NX : 12 + NX, 8 : 8 + NY, :]]
        gz_x[slot] = deriv_z(jnp.concatenate(planes, axis=0), matrix)
    for slot, c in enumerate((1, 2)):
        rows = [ext[c, 8 : 8 + NX, 4:8, :], ext[c, 8 : 8 + NX, 8 + NY : 12 + NY, :]]
        gz_y[slot] = deriv_z(jnp.concatenate(rows, axis=1), matrix)

    def halo_plane(i, carry):
        x = jnp.where(i < 4, i, i + NX)
        xe = x + 4
        lam, mu = lm[0, x], lm[1, x]
        g00 = deriv_x(ext, 0, xe, 8, NY)
        g11 = deriv_y(ext, 1, xe, 8, NY)
        sx[0, x] = lam * (g00 + g11 + gz_x[1, i]) + mu * (g00 + g00)
        sx[1, x] = mu * (deriv_x(ext, 1, xe, 8, NY) + deriv_y(ext, 0, xe, 8, NY))
        sx[2, x] = mu * (deriv_x(ext, 2, xe, 8, NY) + gz_x[0, i])
        return carry

    lax.fori_loop(0, 8, halo_plane, 0)

    def plane(x, carry):
        xe = x + 8
        lam, mu = lm[0, x + 4], lm[1, x + 4]
        e = all_strain(ext, xe, [gz[j, x] for j in range(3)])
        for slot in range(6):
            strain[slot, x] = e[slot]
        pressure = lam * (0.5 * (e[0] + e[3] + e[5]))
        sx[0, x + 4] = pressure + mu * e[0]
        shear = mu * e[1]
        sx[1, x + 4] = shear
        sy[0, x, 8 : 8 + NY, :] = shear
        shear = mu * e[2]
        sx[2, x + 4] = shear
        gz[0, x] = shear
        sy[1, x, 8 : 8 + NY, :] = pressure + mu * e[3]
        shear = mu * e[4]
        sy[2, x, 8 : 8 + NY, :] = shear
        gz[1, x] = shear
        gz[2, x] = pressure + mu * e[5]
        for side, y0 in ((0, 4), (1, 8 + NY)):
            both = lmy[side, x]
            lam4, mu4 = both[:4], both[4:]
            g00 = deriv_x(ext, 0, xe, y0, 4)
            g11 = deriv_y(ext, 1, xe, y0, 4)
            rows = slice(4 * side, 4 * side + 4)
            sy[0, x, y0 : y0 + 4, :] = mu4 * (
                deriv_x(ext, 1, xe, y0, 4) + deriv_y(ext, 0, xe, y0, 4)
            )
            sy[1, x, y0 : y0 + 4, :] = lam4 * (g00 + g11 + gz_y[1, x, rows, :]) + mu4 * (g11 + g11)
            sy[2, x, y0 : y0 + 4, :] = mu4 * (
                deriv_y(ext, 2, xe, y0, 4) + gz_y[0, x, rows, :]
            )
        return carry

    lax.fori_loop(0, NX, plane, 0)
    for c in range(3):
        div[c] = deriv_z(gz[c], matrix)

    def close(x, carry):
        for c in range(3):
            div[c, x] = div[c, x] + (
                deriv_x(sx, c, x + 4, 0, NY) + deriv_y(sy, c, x, 8, NY)
            )
        return carry

    lax.fori_loop(0, NX, close, 0)


def locate(cell):
    plane = lax.axis_size("gy") * NY * NZ
    ix = lax.div(cell, plane) - lax.axis_index("gx") * NX
    iy = lax.rem(lax.div(cell, NZ), lax.axis_size("gy") * NY) - lax.axis_index("gy") * NY
    iz = lax.rem(cell, NZ)
    inside = (ix >= 0) & (ix < NX) & (iy >= 0) & (iy < NY)
    return ix, iy, iz, inside


def add_force(div, c, ix, iy, iz, amount):
    lane = lax.broadcasted_iota(jnp.int32, (1, NZ), 1)
    row = div[c, ix, pl.ds(iy, 1), :]
    div[c, ix, pl.ds(iy, 1), :] = row + jnp.where(lane == iz, amount, 0.0)


def add_source(div, station, wavelet, start, offset):
    ix, iy, iz, inside = locate(station[0])

    @pl.when(inside)
    def _():
        add_force(div, 2, ix, iy, iz, wavelet[0, start[0] + offset])


def add_receivers(div, cells, counts, traces, start, offset):
    moment = start[0] + offset
    time = lax.broadcasted_iota(jnp.int32, (3, traces.shape[2]), 1)

    def one(r, carry):
        ix, iy, iz, inside = locate(cells[0, r])

        @pl.when(inside)
        def _():
            amounts = jnp.sum(
                jnp.where(time == moment, traces[:, r, :], 0.0), axis=1, keepdims=True
            )
            for c in range(3):
                add_force(div, c, ix, iy, iz, amounts[c : c + 1])

        return carry

    lax.fori_loop(0, counts[0], one, 0)


def advance(now, old, div, rho, out, dot_with, dotted):
    def plane(x, carry):
        inverse = 1.0 / rho[x]
        summed = None
        for c in range(3):
            accel = div[c, x] * inverse
            if out is not None:
                out[c, x] = (2.0 * now[c, x] - old[c, x]) + (STEP_DT * STEP_DT) * accel
            if dotted is not None:
                term = dot_with[c, x] * accel
                summed = term if summed is None else summed + term
        if dotted is not None:
            dotted(x, summed)
        return carry

    lax.fori_loop(0, NX, plane, 0)


FIELD_SCRATCH = (
    pltpu.VMEM((3, NX + 16, NY + 16, NZ), F32),
    pltpu.VMEM((2, NX + 8, NY, NZ), F32),
    pltpu.VMEM((2, NX, 8, NZ), F32),
    pltpu.VMEM((3, NX + 8, NY, NZ), F32),
    pltpu.VMEM((3, NX, NY + 16, NZ), F32),
    pltpu.VMEM((3, NX, NY, NZ), F32),
    pltpu.VMEM((3, NX, NY, NZ), F32),
    pltpu.VMEM((2, 8, NY, NZ), F32),
    pltpu.VMEM((2, NX, 8, NZ), F32),
)


def first_s(
    start, station, wavelet, s, bulk_e, bulk_o, rows_e, rows_o, par_e, par_o,
    vp, vs, rho, old, a, s1, strain, k_rho, ext, lm, lmy, sx, sy, div, *depth,
):
    fill_field(ext, s, (bulk_e, bulk_o), (rows_e, rows_o), 0)
    fill_corner(ext, (par_e, par_o), 0)
    fill_lame(lm, lmy, vp, vs, rho, (par_e, par_o), (rows_e, rows_o))
    divergence(ext, lm, lmy, sx, sy, div, strain, *depth)
    add_source(div, station, wavelet, start, 1)

    def keep(x, value):
        k_rho[x] = value

    advance(s, old, div, rho, s1, a, keep)


def first_a(
    start, cells, counts, traces, a, bulk_e, bulk_o, rows_e, rows_o, par_e, par_o,
    vp, vs, rho, old, strain_s, a1, k_two, edge_e, edge_o,
    ext, lm, lmy, sx, sy, div, gz, gz_x, gz_y, strain,
):
    fill_field(ext, a, (bulk_e, bulk_o), (rows_e, rows_o), 3 * NX)
    fill_corner(ext, (par_e, par_o), 8)
    fill_lame(lm, lmy, vp, vs, rho, (par_e, par_o), (rows_e, rows_o))
    divergence(ext, lm, lmy, sx, sy, div, strain, gz, gz_x, gz_y)
    add_receivers(div, cells, counts, traces, start, 1)
    advance(a, old, div, rho, a1, None, None)
    right = even("gx")
    for c in range(3):
        for i in range(4):
            high, low = a1[c, NX - 4 + i], a1[c, i]
            edge_e[c, i] = jnp.where(right, high, low)
            edge_o[c, i] = jnp.where(right, low, high)

    def products(x, carry):
        e_a = [strain[slot, x] for slot in range(6)]
        e_s = [strain_s[slot, x] for slot in range(6)]
        lam, mu = correlate(e_a, e_s)
        k_two[0, x] = lam
        k_two[1, x] = mu
        return carry

    lax.fori_loop(0, NX, products, 0)


def correlate(e_a, e_s):
    trace_a = e_a[0] + e_a[3] + e_a[5]
    trace_s = e_s[0] + e_s[3] + e_s[5]
    mu = 0.5 * (e_a[0] * e_s[0] + e_a[3] * e_s[3] + e_a[5] * e_s[5])
    mu = mu + (e_a[1] * e_s[1] + e_a[2] * e_s[2] + e_a[4] * e_s[4])
    return 0.25 * (trace_a * trace_s), mu


def second_s(
    start, station, wavelet, s, bulk_e, bulk_o, rows_e, rows_o, first_e, first_o, par_e, par_o,
    vp, vs, rho, a, k_rho_first, strain, k_rho, ext, lm, lmy, sx, sy, div, *depth,
):
    fill_field(ext, s, (bulk_e, bulk_o), (rows_e, rows_o), 0)
    fill_rim(ext, (rows_e, rows_o))
    fill_lame(lm, lmy, vp, vs, rho, (par_e, par_o), (first_e, first_o))
    divergence(ext, lm, lmy, sx, sy, div, strain, *depth)
    add_source(div, station, wavelet, start, 0)

    def keep(x, value):
        k_rho[x] = k_rho_first[x] + value

    advance(s, None, div, rho, None, a, keep)


def second_a(parts, a, edge_e, edge_o, got_e, got_o, vp, vs, rho, strain_s, k_two, k_rho, *rest):
    outs, (ext, kernels) = rest[:parts], rest[parts:]
    matrix = band()
    ext[:, 4 : 4 + NX, 8 : 8 + NY, :] = a[...]

    def put_x(left, right):
        ext[:, 0:4, 8 : 8 + NY, :] = left[...]
        ext[:, 4 + NX : 8 + NX, 8 : 8 + NY, :] = right[...]

    ordered("gx", edge_e, edge_o, put_x)

    def put_rows(below, above):
        for c in range(3):
            for i in range(4):
                at = FOUR + c * 4 + i
                ext[c, 4 + i, 4:8, :] = below[at][:4]
                ext[c, 8 + i, 4:8, :] = below[at][4:]
                ext[c, 4 + i, 8 + NY : 12 + NY, :] = above[at][:4]
                ext[c, 8 + i, 8 + NY : 12 + NY, :] = above[at][4:]

    ordered("gy", got_e, got_o, put_rows)

    for c in range(3):
        kernels[c] = deriv_z(a[c], matrix)

    def plane(x, carry):
        e_a = all_strain(ext, x + 4, [kernels[j, x] for j in range(3)])
        lam, mu = correlate(e_a, [strain_s[slot, x] for slot in range(6)])
        lam = STEP_DT * (k_two[0, x] + lam)
        mu = STEP_DT * (k_two[1, x] + mu)
        density = rho[x]
        square_p, square_s = vp[x] * vp[x], vs[x] * vs[x]
        kernels[0, x] = 2.0 * density * square_p * lam
        kernels[1, x] = 2.0 * density * square_s * (mu - 2.0 * lam)
        kernels[2, x] = density * (
            STEP_DT * k_rho[x] + (square_p - 2.0 * square_s) * lam + square_s * mu
        )
        return carry

    lax.fori_loop(0, NX, plane, 0)
    share = NZ // parts
    lane = lax.broadcasted_iota(jnp.int32, (NY, NZ), 1)
    me = lax.axis_index("ens")
    for k in range(parts):
        first = share * jnp.bitwise_xor(me, k)

        def group(i, carry):
            kind, g = lax.div(i, NX // parts), lax.rem(i, NX // parts)
            packed = None
            for j in range(parts):
                shift = lax.rem(share * j - first + NZ, NZ)
                moved = pltpu.roll(kernels[kind, g * parts + j], shift, 1)
                packed = moved if packed is None else jnp.where(lane < share * j, packed, moved)
            outs[k][kind, g] = packed
            return carry

        lax.fori_loop(0, 3 * (NX // parts), group, 0)


def finish(parts, *refs):
    got, outs = refs[:parts], refs[parts:]
    share = NZ // parts
    for kind in range(3):
        for g in range(NX // parts):
            summed = got[0][kind, g]
            for k in range(1, parts):
                summed = summed + got[k][kind, g]
            for j in range(parts):
                moved = summed if j == 0 else pltpu.roll(summed, NZ - share * j, 1)
                outs[kind][g * parts + j] = moved[:, :share]


def swap(value, axis, odd):
    count = lax.axis_size(axis)
    pairs = [(i, i + 1) for i in range(odd, count - 1, 2)]
    return lax.ppermute(value, axis, pairs + [(j, i) for i, j in pairs])


def on_device(
    forward_now, forward_next, adjoint_now, adjoint_prev, speed_p, speed_s, density,
    station_cells, wavelets, receiver_cells, receiver_counts, adjoint_traces, start_step,
):
    s, old_s = forward_now[0], forward_next[0]
    a, old_a = adjoint_now[0], adjoint_prev[0]
    model = (speed_p, speed_s, density)
    start = start_step.reshape(1)
    work = 100_000_000
    tile = shapes(3, NX, NY, NZ)
    rows = call(
        pack_y, (shapes(7 * NX, 8, NZ),) * 2, s, a, *model,
        scratch=(pltpu.VMEM((2, 3, NX, 8, NZ), F32), pltpu.SemaphoreType.DMA((18,))),
        hbm=range(5), vmem=60,
    )
    rows = swap(rows[0], "gy", 0), swap(rows[1], "gy", 1)
    s_e, s_o = swap(s, "gx", 0), swap(s, "gx", 1)
    traces = adjoint_traces[0].transpose(1, 0, 2)
    sources = (station_cells, wavelets, receiver_cells, receiver_counts)
    par = call(
        pack_x, (shapes(48, 8, NZ),) * 2, *rows, *model, *sources, traces, smem=(5, 6, 7, 8)
    )
    a_sent = lax.optimization_barrier((a, par))[0]
    par = swap(par[0], "gx", 0), swap(par[1], "gx", 1)
    a_e, a_o = swap(a_sent, "gx", 0), swap(a_sent, "gx", 1)
    s1, strain_s, k_rho = call(
        first_s, (tile, shapes(6, NX, NY, NZ), shapes(NX, NY, NZ)),
        start, station_cells, wavelets, s, s_e, s_o, *rows, *par, *model, old_s, a,
        scratch=FIELD_SCRATCH, smem=(0, 1, 2), flops=work,
    )
    s1, a_e, a_o = lax.optimization_barrier((s1, a_e, a_o))
    s1_e, s1_o = swap(s1, "gx", 0), swap(s1, "gx", 1)
    edge = shapes(3, 4, NY, NZ)
    a1, k_two, edge_e, edge_o = call(
        first_a, (tile, shapes(2, NX, NY, NZ), edge, edge),
        start, receiver_cells, receiver_counts, traces,
        a, a_e, a_o, *rows, *par, *model, old_a, strain_s,
        scratch=FIELD_SCRATCH + (pltpu.VMEM((6, NX, NY, NZ), F32),), smem=(0, 1, 2), flops=work,
    )
    a1_e, a1_o = swap(edge_e, "gx", 0), swap(edge_o, "gx", 1)
    rim = call(pack_second, (shapes(FOUR + 12, 8, NZ),) * 2, s1, a1, s1_e, s1_o)
    rim = swap(rim[0], "gy", 0), swap(rim[1], "gy", 1)
    strain_s1, k_rho = call(
        second_s, (shapes(6, NX, NY, NZ), shapes(NX, NY, NZ)),
        start, station_cells, wavelets, s1, s1_e, s1_o, *rim, *rows, *par, *model, a1, k_rho,
        scratch=FIELD_SCRATCH, smem=(0, 1, 2), flops=work,
    )
    parts = lax.axis_size("ens")
    pieces = call(
        functools.partial(second_a, parts), (shapes(3, NX // parts, NY, NZ),) * parts,
        a1, a1_e, a1_o, *rim, *model, strain_s1, k_two, k_rho,
        scratch=(pltpu.VMEM((3, NX + 8, NY + 16, NZ), F32), pltpu.VMEM((3, NX, NY, NZ), F32)),
        flops=work,
    )
    far = lax.ppermute(pieces[2], "ens", [(i, i ^ 2) for i in range(parts)])
    near = lax.optimization_barrier((pieces[1], pieces[3]))
    got = [
        pieces[0],
        lax.ppermute(near[0], "ens", [(i, i ^ 1) for i in range(parts)]),
        far,
        lax.ppermute(near[1], "ens", [(i, i ^ 3) for i in range(parts)]),
    ]
    return tuple(
        call(functools.partial(finish, parts), (shapes(NX, NY, NZ // parts),) * 3, *got)
    )


def solution(mesh):
    return jax.shard_map(
        on_device,
        mesh=mesh,
        in_specs=(
            P("ens", None, "gx", "gy", None),
            P("ens", None, "gx", "gy", None),
            P("ens", None, "gx", "gy", None),
            P("ens", None, "gx", "gy", None),
            P("gx", "gy", None),
            P("gx", "gy", None),
            P("gx", "gy", None),
            P("ens"),
            P("ens", None),
            P("ens", None),
            P("ens"),
            P("ens", None, None, None),
            P(),
        ),
        out_specs=(P("gx", "gy", "ens"), P("gx", "gy", "ens"), P("gx", "gy", "ens")),
        check_vma=False,
    )
```
